512 devices in a mesh: src: 64 (over z_lo, y, core), sub: 8 (over x, z_hi).
Axes of the slice: x: 4, y: 8, z: 8 (z_hi: 2, z_lo: 4; z = z_hi * 4 + z_lo), core: 2. Of those that a mesh axis runs over, the one named last changes fastest.
Arguments:
- child_rhs: float32 [8, 1024, 16384], P('sub', None, 'src'), may hold values from -6 to 6
- root_rhs: float32 [2048, 16384], P('sub', 'src'), may hold values from -6 to 6
- child_inverse: bfloat16 [8, 1024, 1024], P('sub', 'src'), as said below
- coupling_block: bfloat16 [8, 1024, 1024], P('sub', 'src'), may hold values from -0.1875 to 0.1875
- root_inverse: bfloat16 [2048, 2048], P('sub', 'src'), as said below
- child_orders: int32 [8], P('sub'), may hold values from 716 to 1024, as said below
- coupling_rows: int32 [8, 1024], P('sub'), may hold values from 0 to 2047, as said below
Outputs:
- child_solution: float32 [8, 1024, 16384], P('sub', None, 'src')
- root_solution: float32 [2048, 16384], P('sub', 'src')
The draws below stay inside these ranges and needn't reach their ends.
Inputs may be any that keep to these rules, and one draw needn't show every extreme that they name: Each child_inverse[j] is lower triangular: zero above the diagonal, diagonal entries between 0.8 and 1.25. `root_inverse`: lower triangular: zero above the diagonal, diagonal entries between 0.8 and 1.25. `coupling_rows`: each row holds 1024 distinct root rows in increasing order. `child_orders`: some child has order 1024.
All inputs are finite; a program needn't handle non-finite values.
Results may differ from the reference program's by a relative error of at most 0.0093.
Values may be sent and summed in bfloat16 or wider, within the bound.
No kernel may reach another device: no remote copies, remote signals or barrier semaphores. Data moves between devices by JAX's collectives and lax.ppermute only.
A program may use at most 64 MiB of HBM per device.

```python
import math
import jax
import jax.numpy as jnp

S0 = 2048
S1 = 1024
K = 1024
CHILDREN = 8
SOURCES = 16384


def lower_factor(key, batch_count, matrix_order):
    key_off, key_diag = jax.random.split(key)
    spread = jnp.clip(jax.random.normal(key_off, (batch_count, matrix_order, matrix_order), jnp.float32), -6.0, 6.0)
    diagonal = jax.random.uniform(key_diag, (batch_count, matrix_order), jnp.float32, 0.8, 1.25)
    positions = jnp.arange(matrix_order)
    strict_lower = positions[:, None] > positions[None, :]
    on_diagonal = positions[:, None] == positions[None, :]
    factor = jnp.where(strict_lower, spread * (0.5 / math.sqrt(matrix_order)), 0.0)
    return factor + jnp.where(on_diagonal, diagonal[:, :, None], 0.0)


def draw_child_inverse(key, part):
    return lower_factor(jax.random.fold_in(key, 11), CHILDREN, S1).astype(jnp.bfloat16)


def draw_root_inverse(key, part):
    return lower_factor(jax.random.fold_in(key, 12), 1, S0)[0].astype(jnp.bfloat16)


def draw_coupling_rows(key, part):

    def choose_rows(child_number):
        shuffled = jax.random.permutation(jax.random.fold_in(jax.random.fold_in(key, 13), child_number), S0)
        return jnp.sort(shuffled[:K])
    return jax.vmap(choose_rows)(jnp.arange(CHILDREN)).astype(jnp.int32)


def draw_child_orders(key, part):
    orders = jax.random.randint(jax.random.fold_in(key, 14), (CHILDREN,), 7 * S1 // 10, S1 + 1, jnp.int32)
    largest = jax.random.randint(jax.random.fold_in(key, 15), (), 0, CHILDREN, jnp.int32)
    return jnp.where(jnp.arange(CHILDREN, dtype=jnp.int32) == largest, S1, orders).astype(jnp.int32)


def block_levels(rng, extent, cuts, smallest, high):
    def one(dim, shards_of):
        heights = jax.random.uniform(jax.random.fold_in(jax.random.fold_in(rng, 6), dim), (shards_of,), jnp.float32, smallest / len(cuts), high / len(cuts))
        return jnp.repeat(jnp.exp(heights), extent[dim] // shards_of).reshape((-1,) + (1,) * (len(extent) - dim - 1))

    loudness = one(*cuts[0])
    for cut in cuts[1:]:
        loudness = loudness * one(*cut)
    return loudness


def bell_draw(stream_key, shape, scale, limit, shards=(), held_as=jnp.bfloat16):
    values = scale * jax.random.normal(stream_key, shape, jnp.float32)
    if shards:
        values = values * block_levels(stream_key, shape, shards, -0.22, 0.18)
    return jnp.clip(values, -limit, limit).astype(held_as)


def setup_inputs(seed: int = 0) -> dict:
    keys = jax.random.split(jax.random.key(seed), 8)
    return {
        "child_rhs": bell_draw(keys[0], (CHILDREN, S1, SOURCES), 1.0, 6.0, ((0, 8), (2, 64)), jnp.float32),
        "root_rhs": bell_draw(keys[1], (S0, SOURCES), 1.0, 6.0, ((0, 8), (1, 64)), jnp.float32),
        "child_inverse": draw_child_inverse(jax.random.fold_in(keys[7], 71), 0),
        "coupling_block": bell_draw(keys[3], (CHILDREN, K, S1), S1 ** -0.5, 0.1875, ((0, 8), (1, 64))),
        "root_inverse": draw_root_inverse(jax.random.fold_in(keys[7], 71), 0),
        "child_orders": draw_child_orders(jax.random.fold_in(keys[7], 71), 0),
        "coupling_rows": draw_coupling_rows(jax.random.fold_in(keys[7], 71), 0),
    }


def reference(child_rhs, root_rhs, child_inverse, coupling_block, root_inverse, child_orders, coupling_rows):
    positions = jnp.arange(S1, dtype=jnp.int32)
    update_total = jnp.zeros(root_rhs.shape, jnp.float32)
    solved_list = []
    for child in range(CHILDREN):
        alive = (positions < child_orders[child])[:, None]
        child_source = jnp.where(alive, child_rhs[child], 0.0).astype(jnp.bfloat16)
        solved = jnp.where(alive, jnp.dot(child_inverse[child], child_source, preferred_element_type=jnp.float32), 0.0)
        solved_list.append(solved)
        update = jnp.dot(coupling_block[child], solved.astype(jnp.bfloat16), preferred_element_type=jnp.float32)
        update_total = update_total.at[coupling_rows[child]].add(update)
    root_source = (root_rhs - update_total).astype(jnp.bfloat16)
    root_forward = jnp.dot(root_inverse, root_source, preferred_element_type=jnp.float32)
    root_round = root_forward.astype(jnp.bfloat16)
    root_solution = jnp.dot(root_inverse.T, root_round, preferred_element_type=jnp.float32)
    root_half = root_solution.astype(jnp.bfloat16)
    result_list = []
    for child in range(CHILDREN):
        alive = (positions < child_orders[child])[:, None]
        picked = root_half[coupling_rows[child]]
        pulled = jnp.dot(coupling_block[child].T, picked, preferred_element_type=jnp.float32)
        residue = jnp.where(alive, solved_list[child] - pulled, 0.0).astype(jnp.bfloat16)
        result = jnp.dot(child_inverse[child].T, residue, preferred_element_type=jnp.float32)
        result_list.append(jnp.where(alive, result, 0.0))
    return jnp.stack(result_list), root_solution
```

```python
import jax
import jax.numpy as jnp
from jax import lax
from jax.sharding import Mesh, PartitionSpec as P

ZL, Y, CORE, X, ZH = 4, 8, 2, 4, 2
SRC = ("zl", "y", "core")
SUB = ("x", "zh")
BF = jnp.bfloat16
F32 = jnp.float32


def gather_blocks(x, axis, length):
    return lax.all_to_all(jnp.broadcast_to(x[None], (length, *x.shape)), axis, 0, 0, tiled=True)


def both_cores(x):
    other = lax.ppermute(x, "core", [(0, 1), (1, 0)])
    first = lax.axis_index("core") == 0
    return jnp.stack([jnp.where(first, x, other), jnp.where(first, other, x)], axis=1)


def dot(a, b, ca, cb):
    return lax.dot_general(a, b, (((ca,), (cb,)), ((), ())), preferred_element_type=F32)


def on_device(
    child_rhs, root_rhs, child_inverse, coupling_block, root_inverse, child_orders, coupling_rows
):
    n = child_rhs.shape[2]
    s1 = child_rhs.shape[1]
    q1 = s1 // ZL
    s0 = root_rhs.shape[0] * X * ZH
    q0 = s0 // ZL
    k = coupling_rows.shape[1]
    r1 = child_inverse.shape[1]
    block = root_rhs.shape[0]
    sub = lax.axis_index("x") * ZH + lax.axis_index("zh")
    index = coupling_rows[0]

    pair = jnp.concatenate([child_inverse[0], coupling_block[0]], axis=0)
    by_zl = gather_blocks(pair, "zl", ZL)
    cb = by_zl[:, r1:, :].reshape(ZL * r1, s1)
    tri_rows = jnp.concatenate(
        [by_zl[3, :r1], jnp.concatenate([by_zl[2, :r1, : 3 * q1], by_zl[0, :r1, :q1]], axis=1),
         jnp.concatenate([by_zl[1, : r1 // 2, : 2 * q1], by_zl[1, r1 // 2 : r1, : 2 * q1]], axis=1)], axis=0)
    packed = jnp.concatenate([cb, tri_rows], axis=0)
    w = both_cores(gather_blocks(packed, "y", Y))
    nc = ZL * r1
    coupling = w[:, :, :nc].reshape(Y, CORE, ZL, r1, s1).transpose(2, 0, 1, 3, 4).reshape(k, s1)
    a3 = w[:, :, nc : nc + r1].reshape(q1, s1)
    a20 = w[:, :, nc + r1 : nc + 2 * r1].reshape(q1, s1)
    a1 = w[:, :, nc + 2 * r1 :]
    a1 = jnp.concatenate([a1[..., : 2 * q1], a1[..., 2 * q1 :]], axis=2).reshape(q1, 2 * q1)
    pad = lambda m: jnp.pad(m, ((0, 0), (0, s1 - m.shape[1])))
    inverse = jnp.concatenate([pad(a20[:, 3 * q1 :]), pad(a1), pad(a20[:, : 3 * q1]), a3], axis=0)

    rt = gather_blocks(root_inverse.T, SUB, X * ZH)
    rc = rt.shape[1]
    rt = rt.transpose(1, 0, 2).reshape(rc, s0)
    rt = gather_blocks(rt, "zl", ZL)
    rt = jnp.concatenate([rt[q, :, q * q0 :] for q in range(ZL)], axis=1)
    rt = both_cores(gather_blocks(rt, "y", Y)).reshape(q0, -1)
    starts = [sum(s0 - p * q0 for p in range(q)) for q in range(ZL)]
    rts = [rt[:, starts[q] : starts[q] + s0 - q * q0] for q in range(ZL)]

    alive = (lax.iota(jnp.int32, s1) < child_orders[0])[:, None]
    source = jnp.where(alive, child_rhs[0], 0.0).astype(BF)
    solved = jnp.where(alive, dot(inverse, source, 1, 0), 0.0)
    update_t = dot(solved.astype(BF), coupling, 0, 1).astype(BF)
    onehot = (index[:, None] == lax.iota(jnp.int32, s0)[None, :]).astype(BF)
    placed_t = -dot(update_t, onehot, 1, 0)
    mine = lax.dynamic_slice(placed_t, (0, sub * block), (n, block)) + root_rhs.T
    placed_t = lax.dynamic_update_slice(placed_t, mine, (0, sub * block))
    parts = lax.all_to_all(placed_t.astype(BF).reshape(X * ZH, n // (X * ZH), s0), SUB, 0, 0, tiled=True)
    s_t = jnp.sum(parts.astype(F32), axis=0).astype(BF)

    f_t = None
    for q in range(ZL):
        term = dot(s_t[:, q * q0 : (q + 1) * q0], rts[q], 1, 0)
        f_t = term if f_t is None else jnp.concatenate([f_t[:, : q * q0], f_t[:, q * q0 :] + term], axis=1)
    f_t = f_t.astype(BF)
    x_t = jnp.concatenate([dot(f_t[:, q * q0 :], rts[q], 1, 1) for q in range(ZL)], axis=1)
    x_all = gather_blocks(x_t.astype(BF), SUB, X * ZH).reshape(n, s0)
    root_out = lax.dynamic_slice(x_all, (0, sub * block), (n, block)).T.astype(F32)

    picked_t = dot(x_all, onehot, 1, 1).astype(BF)
    pulled_t = dot(picked_t, coupling, 1, 0)
    residue_t = jnp.where(alive.T, solved.T - pulled_t, 0.0).astype(BF)
    back = dot(inverse, residue_t, 0, 1)
    child_out = jnp.where(alive, back, 0.0)[None]
    return (child_out, root_out)


def solution(mesh):
    fine = Mesh(mesh.devices.reshape(ZL, Y, CORE, X, ZH), (*SRC, *SUB))
    return jax.shard_map(
        on_device,
        mesh=fine,
        in_specs=(
            P(SUB, None, SRC),
            P(SUB, SRC),
            P(SUB, SRC, None),
            P(SUB, SRC, None),
            P(SUB, SRC),
            P(SUB),
            P(SUB, None),
        ),
        out_specs=(P(SUB, None, SRC), P(SUB, SRC)),
        check_vma=False,
    )
```

```python
import jax
import jax.numpy as jnp
from jax import lax
from jax.sharding import Mesh, PartitionSpec as P

ZL, Y, CORE, X, ZH = 4, 8, 2, 4, 2
SRC = ("zl", "y", "core")
SUB = ("x", "zh")
BF = jnp.bfloat16
F32 = jnp.float32


def gather_blocks(x, axis, length):
    return lax.all_to_all(jnp.broadcast_to(x[None], (length, *x.shape)), axis, 0, 0, tiled=True)


def ring(x):
    forth = [(i, (i + 1) % Y) for i in range(Y)]
    back = [(i, (i - 1) % Y) for i in range(Y)]
    here = lax.axis_index("y")
    blocks = jnp.zeros((Y, *x.shape), x.dtype)
    place = lambda blocks, piece, at: lax.dynamic_update_slice(
        blocks, piece[None], (lax.rem(here + at + Y, Y),) + (0,) * x.ndim
    )
    blocks = place(blocks, x, 0)
    up = down = x
    for step in range(1, Y // 2 + 1):
        up = lax.ppermute(up, "y", forth)
        blocks = place(blocks, up, -step)
        if step < Y // 2:
            down = lax.ppermute(down, "y", back)
            blocks = place(blocks, down, step)
    return blocks


def both_cores(x):
    other = lax.ppermute(x, "core", [(0, 1), (1, 0)])
    first = lax.axis_index("core") == 0
    return jnp.stack([jnp.where(first, x, other), jnp.where(first, other, x)], axis=1)


def dot(a, b, ca, cb):
    return lax.dot_general(a, b, (((ca,), (cb,)), ((), ())), preferred_element_type=F32)


def on_device(
    child_rhs, root_rhs, child_inverse, coupling_block, root_inverse, child_orders, coupling_rows
):
    n = child_rhs.shape[2]
    s1 = child_rhs.shape[1]
    q1 = s1 // ZL
    s0 = root_rhs.shape[0] * X * ZH
    q0 = s0 // ZL
    k = coupling_rows.shape[1]
    r1 = child_inverse.shape[1]
    block = root_rhs.shape[0]
    sub = lax.axis_index("x") * ZH + lax.axis_index("zh")
    index = coupling_rows[0]

    pair = jnp.concatenate([child_inverse[0], coupling_block[0]], axis=0)
    by_zl = gather_blocks(jnp.concatenate([pair, root_inverse.T], axis=1), "zl", ZL)
    rt = by_zl[:, :, s1:]
    by_zl = by_zl[:, :, :s1]
    cb = by_zl[:, r1:, :].reshape(ZL * r1, s1)
    tri_rows = jnp.concatenate(
        [by_zl[3, :r1], jnp.concatenate([by_zl[2, :r1, : 3 * q1], by_zl[0, :r1, :q1]], axis=1),
         jnp.concatenate([by_zl[1, : r1 // 2, : 2 * q1], by_zl[1, r1 // 2 : r1, : 2 * q1]], axis=1)], axis=0)
    packed = jnp.concatenate([cb, tri_rows], axis=0)
    w = both_cores(ring(packed))
    nc = ZL * r1
    coupling = w[:, :, :nc].reshape(Y, CORE, ZL, r1, s1).transpose(2, 0, 1, 3, 4).reshape(k, s1)
    a3 = w[:, :, nc : nc + r1].reshape(q1, s1)
    a20 = w[:, :, nc + r1 : nc + 2 * r1].reshape(q1, s1)
    a1 = w[:, :, nc + 2 * r1 :]
    a1 = jnp.concatenate([a1[..., : 2 * q1], a1[..., 2 * q1 :]], axis=2).reshape(q1, 2 * q1)
    pad = lambda m: jnp.pad(m, ((0, 0), (0, s1 - m.shape[1])))
    inverse = jnp.concatenate([pad(a20[:, 3 * q1 :]), pad(a1), pad(a20[:, : 3 * q1]), a3], axis=0)

    rt = gather_blocks(rt, SUB, X * ZH)
    rt = jnp.concatenate([rt[i, q] for q in range(ZL) for i in range(q * q0 // block, X * ZH)], axis=1)
    rt = both_cores(ring(rt)).reshape(q0, -1)
    starts = [sum(s0 - p * q0 for p in range(q)) for q in range(ZL)]
    rts = [rt[:, starts[q] : starts[q] + s0 - q * q0] for q in range(ZL)]

    alive = (lax.iota(jnp.int32, s1) < child_orders[0])[:, None]
    source = jnp.where(alive, child_rhs[0], 0.0).astype(BF)
    solved = jnp.where(alive, dot(inverse, source, 1, 0), 0.0)
    update_t = dot(solved.astype(BF), coupling, 0, 1).astype(BF)
    onehot = (index[:, None] == lax.iota(jnp.int32, s0)[None, :]).astype(BF)
    placed_t = -dot(update_t, onehot, 1, 0)
    mine = lax.dynamic_slice(placed_t, (0, sub * block), (n, block)) + root_rhs.T
    placed_t = lax.dynamic_update_slice(placed_t, mine, (0, sub * block))
    parts = lax.all_to_all(placed_t.astype(BF).reshape(X, n // X, s0), "x", 0, 0, tiled=True)
    part = jnp.sum(parts.astype(F32), axis=0)
    s_t = (part + lax.ppermute(part.astype(BF), "zh", [(0, 1), (1, 0)]).astype(F32)).astype(BF)

    f_t = None
    for q in range(ZL):
        term = dot(s_t[:, q * q0 : (q + 1) * q0], rts[q], 1, 0)
        f_t = term if f_t is None else jnp.concatenate([f_t[:, : q * q0], f_t[:, q * q0 :] + term], axis=1)
    f_t = f_t.astype(BF)
    x_t = jnp.concatenate([dot(f_t[:, q * q0 :], rts[q], 1, 1) for q in range(ZL)], axis=1)
    x_all = gather_blocks(x_t.astype(BF), "x", X).reshape(n, s0)
    root_out = lax.dynamic_slice(x_all, (0, sub * block), (n, block)).T.astype(F32)

    picked_t = dot(x_all, onehot, 1, 1).astype(BF)
    pulled_t = dot(picked_t, coupling, 1, 0)
    residue_t = jnp.where(alive.T, solved.T - pulled_t, 0.0).astype(BF)
    back = dot(inverse, residue_t, 0, 1)
    child_out = jnp.where(alive, back, 0.0)[None]
    return (child_out, root_out)


def solution(mesh):
    fine = Mesh(mesh.devices.reshape(ZL, Y, CORE, X, ZH), (*SRC, *SUB))
    return jax.shard_map(
        on_device,
        mesh=fine,
        in_specs=(
            P(SUB, None, SRC),
            P(SUB, SRC),
            P(SUB, SRC, None),
            P(SUB, SRC, None),
            P(SUB, SRC),
            P(SUB),
            P(SUB, None),
        ),
        out_specs=(P(SUB, None, SRC), P(SUB, SRC)),
        check_vma=False,
    )
```

```python
import jax
import jax.numpy as jnp
from jax import lax
from jax.experimental import pallas as pl
from jax.experimental.pallas import tpu as pltpu
from jax.sharding import Mesh, PartitionSpec as P

ZL, Y, CORE, X, ZH = 4, 8, 2, 4, 2
SRC = ("zl", "y", "core")
SUB = ("x", "zh")
BF = jnp.bfloat16
F32 = jnp.float32
FORTH = [(i, (i + 1) % Y) for i in range(Y)]
BACK = [(i, (i - 1) % Y) for i in range(Y)]
SWAP = [(0, 1), (1, 0)]
FIRST = Y // 2


def gather_blocks(x, axis, length):
    return lax.all_to_all(jnp.broadcast_to(x[None], (length, *x.shape)), axis, 0, 0, tiled=True)


def after(x, *others):
    return lax.optimization_barrier((x, *others))[0]


def dot(a, b, ca=1, cb=0):
    return lax.dot_general(a, b, (((ca,), (cb,)), ((), ())), preferred_element_type=F32)


def onehot(idx_ref, at, width):
    k = idx_ref.shape[0]
    cols = lax.broadcasted_iota(jnp.int32, (k, width), 1) + at
    return jnp.where(idx_ref[...] == cols, 1.0, 0.0).astype(BF)


def by_core(core, mine_ref, other_ref, put):
    @pl.when(core == 0)
    def _():
        put(mine_ref, 0)
        put(other_ref, 1)

    @pl.when(core != 0)
    def _():
        put(other_ref, 0)
        put(mine_ref, 1)


def forward_kernel(
    place_ref, mine_ref, other_ref, rhs_ref, root_ref, idx_ref,
    placed_ref, solved_ref, a_ref, c_ref,
):
    here, core, sub, order = (place_ref[i] for i in range(4))
    s1, n = rhs_ref.shape
    r1 = mine_ref.shape[1]
    q1 = s1 // ZL
    block = root_ref.shape[0]

    def put(blocks_ref, c):
        for j in range(Y):
            y = lax.rem(here + (j - FIRST + Y), Y)
            at = pl.multiple_of(y * (CORE * r1), CORE * r1) + c * r1
            for q in range(ZL):
                c_ref[pl.ds(q * q1 + at, r1), :] = blocks_ref[j, :, q * s1 : (q + 1) * s1]
            left = ZL * s1
            for q in reversed(range(ZL)):
                width = (q + 1) * q1
                a_ref[pl.ds(q * q1 + at, r1), :width] = blocks_ref[j, :, left : left + width]
                left += width

    by_core(core, mine_ref, other_ref, put)
    rows = lax.broadcasted_iota(jnp.int32, (s1, n), 0)
    source = jnp.where(rows < order, rhs_ref[...], 0.0).astype(BF)
    for q in range(ZL):
        top = (q + 1) * q1
        part = dot(a_ref[q * q1 : top, :top], source[:top])
        part = jnp.where(rows[q * q1 : top] < order, part, 0.0)
        solved_ref[:, q * q1 : top] = part.T
    update = dot(solved_ref[...].astype(BF), c_ref[...], 1, 1).astype(BF)
    root = root_ref[...].T
    for b in range(placed_ref.shape[1] // block):
        part = dot(update, onehot(idx_ref, b * block, block))
        placed_ref[:, b * block : (b + 1) * block] = (
            jnp.where(sub == b, root, 0.0) - part
        ).astype(BF)


def root_kernel(place_ref, s_ref, mine_ref, other_ref, last_ref, far_ref, out_ref, r_ref, f_ref):
    here, core = place_ref[0], place_ref[1]
    s0 = s_ref.shape[1]
    q0 = s0 // ZL
    rc = mine_ref.shape[1]

    def rows(j, c):
        y = lax.rem(here + (j - FIRST + Y), Y)
        return pl.ds(pl.multiple_of(y * (CORE * rc), CORE * rc) + c * rc, rc)

    def put(blocks_ref, c):
        for j in range(1, Y):
            r_ref[rows(j, c), :] = blocks_ref[j - 1]

    def put_last(block_ref, c):
        r_ref[rows(0, c), :] = block_ref[...]

    by_core(core, mine_ref, other_ref, put)
    by_core(core, last_ref, far_ref, put_last)
    left = 0
    spans = []
    for q in range(ZL):
        spans.append((left, left + s0 - q * q0))
        left = spans[-1][1]
    for q in range(ZL):
        term = dot(s_ref[:, q * q0 : (q + 1) * q0], r_ref[:, spans[q][0] : spans[q][1]])
        f_ref[:, q * q0 :] = term if q == 0 else f_ref[:, q * q0 :] + term
    f = f_ref[...].astype(BF)
    for q in range(ZL):
        part = dot(f[:, q * q0 :], r_ref[:, spans[q][0] : spans[q][1]], 1, 1).astype(BF)
        for i in range(out_ref.shape[0]):
            out_ref[i, :, q * q0 : (q + 1) * q0] = part


def backward_kernel(place_ref, x_ref, solved_ref, a_ref, c_ref, idx_ref, out_ref, root_ref):
    sub, order = place_ref[2], place_ref[3]
    n, s1 = solved_ref.shape
    q1 = s1 // ZL
    block = root_ref.shape[0]
    picked = None
    for b in range(x_ref.shape[1] // block):
        part = dot(x_ref[:, b * block : (b + 1) * block], onehot(idx_ref, b * block, block), 1, 1)
        picked = part if picked is None else picked + part
    pulled = dot(picked.astype(BF), c_ref[...])
    cols = lax.broadcasted_iota(jnp.int32, (n, s1), 1)
    residue = jnp.where(cols < order, solved_ref[...] - pulled, 0.0).astype(BF)
    rows = lax.broadcasted_iota(jnp.int32, (q1, n), 0)
    for q in range(ZL):
        part = dot(residue[:, q * q1 :], a_ref[q * q1 :, q * q1 : (q + 1) * q1])
        out_ref[q * q1 : (q + 1) * q1, :] = jnp.where(rows + q * q1 < order, part.T, 0.0)
    at = pl.multiple_of(sub * block, block)
    root_ref[...] = x_ref[:, pl.ds(at, block)].astype(F32).T


def call(kernel, outs, args, scratch=(), flops=0):
    moved = sum(a.size * a.dtype.itemsize for a in (*args, *outs))
    vmem = pl.BlockSpec(memory_space=pltpu.VMEM)
    return pl.pallas_call(
        kernel,
        out_shape=outs,
        in_specs=[pl.BlockSpec(memory_space=pltpu.SMEM)] + [vmem] * (len(args) - 1),
        out_specs=[vmem] * len(outs),
        scratch_shapes=scratch,
        cost_estimate=pl.CostEstimate(flops=flops, transcendentals=0, bytes_accessed=moved),
        compiler_params=pltpu.CompilerParams(vmem_limit_bytes=40 << 20),
    )(*args)


def on_device(
    child_rhs, root_rhs, child_inverse, coupling_block, root_inverse, child_orders, coupling_rows
):
    n = child_rhs.shape[2]
    s1 = child_rhs.shape[1]
    q1 = s1 // ZL
    s0 = root_rhs.shape[0] * X * ZH
    q0 = s0 // ZL
    k = coupling_rows.shape[1]
    r1 = child_inverse.shape[1]
    block = root_rhs.shape[0]
    sub = lax.axis_index("x") * ZH + lax.axis_index("zh")
    place = jnp.stack([lax.axis_index("y"), lax.axis_index("core"), sub, child_orders[0]])
    idx = coupling_rows[0][:, None]
    shape = jax.ShapeDtypeStruct

    pair = jnp.concatenate([child_inverse[0], coupling_block[0]], axis=0)
    by_zl = gather_blocks(jnp.concatenate([pair, root_inverse.T], axis=1), "zl", ZL)
    own = jnp.concatenate(
        [by_zl[q, r1:, :s1] for q in range(ZL)]
        + [by_zl[q, :r1, : (q + 1) * q1] for q in reversed(range(ZL))],
        axis=1,
    )
    rt = by_zl[:, :, s1:]
    rc = rt.shape[1]

    up = {1: lax.ppermute(own, "y", FORTH)}
    down = {1: lax.ppermute(own, "y", BACK)}
    rz = lax.ppermute(rt, "zh", SWAP)
    low = lax.axis_index("zh") == 0
    rt = jnp.stack([jnp.where(low, rt, rz), jnp.where(low, rz, rt)])
    up[2] = lax.ppermute(up[1], "y", FORTH)
    down[2] = lax.ppermute(down[1], "y", BACK)
    rt = gather_blocks(after(rt, up[1], down[1]), "x", X)
    up[3] = lax.ppermute(up[2], "y", FORTH)
    down[3] = lax.ppermute(down[2], "y", BACK)
    up[4] = lax.ppermute(up[3], "y", FORTH)
    rt = jnp.concatenate(
        [rt[x, z, q] for q in range(ZL) for x in range(q, X) for z in range(ZH)], axis=1
    )
    rt = after(rt, up[3], down[3])
    rup = {1: lax.ppermute(rt, "y", FORTH)}
    rdown = {1: lax.ppermute(rt, "y", BACK)}
    mine = jnp.stack([up[i] for i in (4, 3, 2, 1)] + [own] + [down[i] for i in (1, 2, 3)])
    other = lax.ppermute(mine, "core", SWAP)
    rup[2] = lax.ppermute(after(rup[1], mine), "y", FORTH)
    rdown[2] = lax.ppermute(after(rdown[1], mine), "y", BACK)

    placed, solved, a, c = call(
        forward_kernel,
        [shape((n, s0), BF), shape((n, s1), F32), shape((s1, s1), BF), shape((k, s1), BF)],
        [place, mine, other, child_rhs[0], root_rhs, idx],
        flops=2 * n * (s1 * s1 + k * s1 + k * s0),
    )
    rup[3] = lax.ppermute(after(rup[2], placed), "y", FORTH)
    rdown[3] = lax.ppermute(after(rdown[2], placed), "y", BACK)
    parts = lax.all_to_all(placed.reshape(X, n // X, s0), "x", 0, 0, tiled=True)
    part = jnp.sum(parts.astype(F32), axis=0)
    sent, r3, d3 = lax.optimization_barrier((part.astype(BF), rup[3], rdown[3]))
    far = lax.ppermute(sent, "zh", SWAP)
    last = lax.ppermute(r3, "y", FORTH)
    rmine = jnp.stack([r3, rup[2], rup[1], rt, rdown[1], rdown[2], d3])
    rother = lax.ppermute(rmine, "core", SWAP)
    s_t = (part + far.astype(F32)).astype(BF)
    rlast = lax.ppermute(last, "core", SWAP)

    x_t, = call(
        root_kernel,
        [shape((X, n // X, s0), BF)],
        [place, s_t, rmine, rother, last, rlast],
        [pltpu.VMEM((q0, rt.shape[1]), BF), pltpu.VMEM((n // X, s0), F32)],
        flops=4 * (n // X) * q0 * rt.shape[1],
    )
    x_all = lax.all_to_all(x_t, "x", 0, 0, tiled=True).reshape(n, s0)

    child_out, root_out = call(
        backward_kernel,
        [shape((s1, n), F32), shape((block, n), F32)],
        [place, x_all, solved, a, c, idx],
        flops=2 * n * (s1 * s1 + k * s1 + k * s0),
    )
    return (child_out[None], root_out)


def solution(mesh):
    fine = Mesh(mesh.devices.reshape(ZL, Y, CORE, X, ZH), (*SRC, *SUB))
    return jax.shard_map(
        on_device,
        mesh=fine,
        in_specs=(
            P(SUB, None, SRC),
            P(SUB, SRC),
            P(SUB, SRC, None),
            P(SUB, SRC, None),
            P(SUB, SRC),
            P(SUB),
            P(SUB, None),
        ),
        out_specs=(P(SUB, None, SRC), P(SUB, SRC)),
        check_vma=False,
    )
```

```python
import jax
import jax.numpy as jnp
from jax import lax
from jax.experimental import pallas as pl
from jax.experimental.pallas import tpu as pltpu
from jax.sharding import Mesh, PartitionSpec as P

ZL, Y, CORE, X, ZH = 4, 8, 2, 4, 2
SRC = ("zl", "y", "core")
SUB = ("x", "zh")
BF = jnp.bfloat16
F32 = jnp.float32
FORTH = [(i, (i + 1) % Y) for i in range(Y)]
BACK = [(i, (i - 1) % Y) for i in range(Y)]
SWAP = [(0, 1), (1, 0)]
EARLY, LATE = (0, -1, 1, -2, 2), (-3, 3, -4)


def gather_blocks(x, axis, length):
    return lax.all_to_all(jnp.broadcast_to(x[None], (length, *x.shape)), axis, 0, 0, tiled=True)


def after(x, *others):
    return lax.optimization_barrier((x, *others))[0]


def dot(a, b, ca=1, cb=0):
    return lax.dot_general(a, b, (((ca,), (cb,)), ((), ())), preferred_element_type=F32)


def onehot(idx_ref, at, width):
    k = idx_ref.shape[0]
    cols = lax.broadcasted_iota(jnp.int32, (k, width), 1) + at
    return jnp.where(idx_ref[...] == cols, 1.0, 0.0).astype(BF)


def by_core(core, early, late, put):
    for mine, other in ((0, 1), (1, 0)):

        @pl.when(core == mine)
        def _():
            for blocks, steps in ((early, EARLY), (late, LATE)):
                put(blocks[0], steps, mine)
                put(blocks[1], steps, other)


def child_weights(here, core, early, late, a_ref, c_ref):
    s1 = a_ref.shape[0]
    r1 = early[0].shape[1]
    q1 = s1 // ZL

    def put(blocks_ref, steps, c):
        for j, step in enumerate(steps):
            y = lax.rem(here + (step + Y), Y)
            at = pl.multiple_of(y * (CORE * r1), CORE * r1) + c * r1
            for q in range(ZL):
                c_ref[pl.ds(q * q1 + at, r1), :] = blocks_ref[j, :, q * s1 : (q + 1) * s1]
            left = ZL * s1
            for q in reversed(range(ZL)):
                width = (q + 1) * q1
                a_ref[pl.ds(q * q1 + at, r1), :width] = blocks_ref[j, :, left : left + width]
                left += width

    by_core(core, early, late, put)


def forward_kernel(
    place_ref, early_ref, early_far_ref, late_ref, late_far_ref, rhs_ref, root_ref, idx_ref,
    placed_ref, out_ref, solved_ref, a_ref, c_ref, sem,
):
    here, core, sub, order = (place_ref[i] for i in range(4))
    s1, n = rhs_ref.shape
    q1 = s1 // ZL
    block = root_ref.shape[0]
    child_weights(here, core, (early_ref, early_far_ref), (late_ref, late_far_ref), a_ref, c_ref)
    rows = lax.broadcasted_iota(jnp.int32, (s1, n), 0)
    source = jnp.where(rows < order, rhs_ref[...], 0.0).astype(BF)
    for q in range(ZL):
        top = (q + 1) * q1
        part = dot(a_ref[q * q1 : top, :top], source[:top])
        part = jnp.where(rows[q * q1 : top] < order, part, 0.0)
        solved_ref[:, q * q1 : top] = part.T
    copy = pltpu.make_async_copy(solved_ref, out_ref, sem)
    copy.start()
    update = dot(solved_ref[...].astype(BF), c_ref[...], 1, 1).astype(BF)
    root = root_ref[...].T
    for b in range(placed_ref.shape[1] // block):
        part = dot(update, onehot(idx_ref, b * block, block))
        placed_ref[:, b * block : (b + 1) * block] = (
            jnp.where(sub == b, root, 0.0) - part
        ).astype(BF)
    copy.wait()


def root_kernel(
    place_ref, s_ref, early_ref, early_far_ref, late_ref, late_far_ref, out_ref, r_ref, f_ref
):
    here, core = place_ref[0], place_ref[1]
    s0 = s_ref.shape[1]
    q0 = s0 // ZL
    half, width = r_ref.shape[0] // (Y * CORE * 2), r_ref.shape[1]

    def put(blocks_ref, steps, c):
        for j, step in enumerate(steps):
            y = lax.rem(here + (step + Y), Y)
            at = pl.multiple_of(y * (CORE * 2 * half), CORE * 2 * half) + c * 2 * half
            for h in range(2):
                r_ref[pl.ds(at + h * half, half), :] = blocks_ref[
                    j, :, h * width : (h + 1) * width
                ]

    by_core(core, (early_ref, early_far_ref), (late_ref, late_far_ref), put)
    left = 0
    spans = []
    for q in range(ZL):
        spans.append((left, left + s0 - q * q0))
        left = spans[-1][1]
    for q in range(ZL):
        term = dot(s_ref[:, q * q0 : (q + 1) * q0], r_ref[:, spans[q][0] : spans[q][1]])
        f_ref[:, q * q0 :] = term if q == 0 else f_ref[:, q * q0 :] + term
    f = f_ref[...].astype(BF)
    for q in range(ZL):
        part = dot(f[:, q * q0 :], r_ref[:, spans[q][0] : spans[q][1]], 1, 1).astype(BF)
        for i in range(out_ref.shape[0]):
            out_ref[i, :, q * q0 : (q + 1) * q0] = part


def backward_kernel(
    place_ref, x_ref, in_ref, early_ref, early_far_ref, late_ref, late_far_ref, idx_ref,
    out_ref, root_ref, solved_ref, a_ref, c_ref, sem,
):
    here, core, sub, order = (place_ref[i] for i in range(4))
    copy = pltpu.make_async_copy(in_ref, solved_ref, sem)
    copy.start()
    child_weights(here, core, (early_ref, early_far_ref), (late_ref, late_far_ref), a_ref, c_ref)
    n, s1 = solved_ref.shape
    q1 = s1 // ZL
    block = root_ref.shape[0]
    picked = None
    for b in range(x_ref.shape[1] // block):
        part = dot(x_ref[:, b * block : (b + 1) * block], onehot(idx_ref, b * block, block), 1, 1)
        picked = part if picked is None else picked + part
    pulled = dot(picked.astype(BF), c_ref[...])
    cols = lax.broadcasted_iota(jnp.int32, (n, s1), 1)
    copy.wait()
    residue = jnp.where(cols < order, solved_ref[...] - pulled, 0.0).astype(BF)
    rows = lax.broadcasted_iota(jnp.int32, (q1, n), 0)
    for q in range(ZL):
        part = dot(residue[:, q * q1 :], a_ref[q * q1 :, q * q1 : (q + 1) * q1])
        out_ref[q * q1 : (q + 1) * q1, :] = jnp.where(rows + q * q1 < order, part.T, 0.0)
    at = pl.multiple_of(sub * block, block)
    root_ref[...] = x_ref[:, pl.ds(at, block)].astype(F32).T


def call(kernel, outs, args, scratch=(), flops=0, far=((), ())):
    moved = sum(a.size * a.dtype.itemsize for a in (*args, *outs))
    vmem = pl.BlockSpec(memory_space=pltpu.VMEM)
    hbm = pl.BlockSpec(memory_space=pltpu.HBM)
    return pl.pallas_call(
        kernel,
        out_shape=outs,
        in_specs=[pl.BlockSpec(memory_space=pltpu.SMEM)]
        + [hbm if i in far[0] else vmem for i in range(1, len(args))],
        out_specs=[hbm if i in far[1] else vmem for i in range(len(outs))],
        scratch_shapes=scratch,
        cost_estimate=pl.CostEstimate(flops=flops, transcendentals=0, bytes_accessed=moved),
        compiler_params=pltpu.CompilerParams(vmem_limit_bytes=20 << 20),
    )(*args)


def on_device(
    child_rhs, root_rhs, child_inverse, coupling_block, root_inverse, child_orders, coupling_rows
):
    n = child_rhs.shape[2]
    s1 = child_rhs.shape[1]
    q1 = s1 // ZL
    s0 = root_rhs.shape[0] * X * ZH
    q0 = s0 // ZL
    k = coupling_rows.shape[1]
    r1 = child_inverse.shape[1]
    block = root_rhs.shape[0]
    sub = lax.axis_index("x") * ZH + lax.axis_index("zh")
    place = jnp.stack([lax.axis_index("y"), lax.axis_index("core"), sub, child_orders[0]])
    idx = coupling_rows[0][:, None]
    shape = jax.ShapeDtypeStruct

    pair = jnp.concatenate([child_inverse[0], coupling_block[0]], axis=0)
    by_zl = gather_blocks(jnp.concatenate([pair, root_inverse.T], axis=1), "zl", ZL)
    own = jnp.concatenate(
        [by_zl[q, r1:, :s1] for q in range(ZL)]
        + [by_zl[q, :r1, : (q + 1) * q1] for q in reversed(range(ZL))],
        axis=1,
    )
    rt = after(by_zl[:, :, s1:], own)
    width = own.shape[1]

    up = {1: lax.ppermute(own, "y", FORTH)}
    down = {1: lax.ppermute(own, "y", BACK)}
    rz = lax.ppermute(rt, "zh", SWAP)
    low = lax.axis_index("zh") == 0
    rt = jnp.stack([jnp.where(low, rt, rz), jnp.where(low, rz, rt)])
    up[2] = lax.ppermute(up[1], "y", FORTH)
    down[2] = lax.ppermute(down[1], "y", BACK)
    rt = gather_blocks(rt, "x", X)
    half = own.shape[0]
    rt = jnp.concatenate(
        [
            rt[x, z, q, h * half : (h + 1) * half]
            for h in range(2) for q in range(ZL) for x in range(q, X) for z in range(ZH)
        ],
        axis=1,
    )
    early = jnp.stack([own, up[1], down[1], up[2], down[2]])
    early_far = lax.ppermute(early, "core", SWAP)
    both_up = lax.ppermute(jnp.concatenate([up[2], rt], axis=1), "y", FORTH)
    both_down = lax.ppermute(jnp.concatenate([down[2], rt], axis=1), "y", BACK)
    both_up2 = lax.ppermute(both_up, "y", FORTH)
    rdown2 = lax.ppermute(both_down[:, width:], "y", BACK)
    late = jnp.stack([both_up[:, :width], both_down[:, :width], both_up2[:, :width]])
    late_far = lax.ppermute(late, "core", SWAP)

    weights = [early, early_far, late, late_far]
    scratch = [pltpu.VMEM((s1, s1), BF), pltpu.VMEM((k, s1), BF)]
    flops = 2 * n * (s1 * s1 + k * s1 + k * s0)
    placed, solved = call(
        forward_kernel,
        [shape((n, s0), BF), shape((n, s1), F32)],
        [place, *weights, child_rhs[0], root_rhs, idx],
        [pltpu.VMEM((n, s1), F32), *scratch, pltpu.SemaphoreType.DMA],
        flops,
        ((), (1,)),
    )
    rup2 = after(both_up2[:, width:], placed)
    rup3 = lax.ppermute(rup2, "y", FORTH)
    rdown3 = lax.ppermute(after(rdown2, placed), "y", BACK)
    rearly = jnp.stack([rt, both_up[:, width:], both_down[:, width:], rup2, rdown2])
    rearly_far = lax.ppermute(rearly, "core", SWAP)
    parts = lax.all_to_all(placed.reshape(X, n // X, s0), "x", 0, 0, tiled=True)
    part = jnp.sum(parts.astype(F32), axis=0)
    far = lax.ppermute(part.astype(BF), "zh", SWAP)
    rup4 = lax.ppermute(rup3, "y", FORTH)
    rlate = jnp.stack([rup3, rdown3, rup4])
    rlate_far = lax.ppermute(rlate, "core", SWAP)
    s_t = (part + far.astype(F32)).astype(BF)

    x_t, = call(
        root_kernel,
        [shape((X, n // X, s0), BF)],
        [place, s_t, rearly, rearly_far, rlate, rlate_far],
        [pltpu.VMEM((q0, rt.shape[1] // 2), BF), pltpu.VMEM((n // X, s0), F32)],
        flops=2 * (n // X) * q0 * rt.shape[1],
    )
    x_all = lax.all_to_all(x_t, "x", 0, 0, tiled=True).reshape(n, s0)

    child_out, root_out = call(
        backward_kernel,
        [shape((s1, n), F32), shape((block, n), F32)],
        [place, x_all, solved, *weights, idx],
        [pltpu.VMEM((n, s1), F32), *scratch, pltpu.SemaphoreType.DMA],
        flops,
        ((2,), ()),
    )
    return (child_out[None], root_out)


def solution(mesh):
    fine = Mesh(mesh.devices.reshape(ZL, Y, CORE, X, ZH), (*SRC, *SUB))
    return jax.shard_map(
        on_device,
        mesh=fine,
        in_specs=(
            P(SUB, None, SRC),
            P(SUB, SRC),
            P(SUB, SRC, None),
            P(SUB, SRC, None),
            P(SUB, SRC),
            P(SUB),
            P(SUB, None),
        ),
        out_specs=(P(SUB, None, SRC), P(SUB, SRC)),
        check_vma=False,
    )
```

```python
import jax
import jax.numpy as jnp
from jax import lax
from jax.experimental import pallas as pl
from jax.experimental.pallas import tpu as pltpu
from jax.sharding import Mesh, PartitionSpec as P

ZL, Y, CORE, X, ZH = 4, 8, 2, 4, 2
SRC = ("zl", "y", "core")
SUB = ("x", "zh")
BF = jnp.bfloat16
F32 = jnp.float32
FORTH = [(i, (i + 1) % Y) for i in range(Y)]
BACK = [(i, (i - 1) % Y) for i in range(Y)]
SWAP = [(0, 1), (1, 0)]
EARLY, LATE = (0, -1, 1, -2, 2), (-3, 3, -4)


def gather_blocks(x, axis, length):
    return lax.all_to_all(jnp.broadcast_to(x[None], (length, *x.shape)), axis, 0, 0, tiled=True)


def after(x, *others):
    return lax.optimization_barrier((x, *others))[0]


def dot(a, b, ca=1, cb=0):
    return lax.dot_general(a, b, (((ca,), (cb,)), ((), ())), preferred_element_type=F32)


def onehot(idx_ref, at, width):
    k = idx_ref.shape[0]
    cols = lax.broadcasted_iota(jnp.int32, (k, width), 1) + at
    return jnp.where(idx_ref[...] == cols, 1.0, 0.0).astype(BF)


def by_core(core, early, late, put):
    for mine, other in ((0, 1), (1, 0)):

        @pl.when(core == mine)
        def _():
            for blocks, steps in ((early, EARLY), (late, LATE)):
                put(blocks[0], steps, mine)
                put(blocks[1], steps, other)


def child_weights(here, core, early, late, a_ref, c_ref):
    s1 = a_ref.shape[0]
    r1 = early[0].shape[1]
    q1 = s1 // ZL

    def put(blocks_ref, steps, c):
        for j, step in enumerate(steps):
            y = lax.rem(here + (step + Y), Y)
            at = pl.multiple_of(y * (CORE * r1), CORE * r1) + c * r1
            for q in range(ZL):
                c_ref[pl.ds(q * q1 + at, r1), :] = blocks_ref[j, :, q * s1 : (q + 1) * s1]
            left = ZL * s1
            for q in reversed(range(ZL)):
                width = (q + 1) * q1
                a_ref[pl.ds(q * q1 + at, r1), :width] = blocks_ref[j, :, left : left + width]
                left += width

    by_core(core, early, late, put)


def forward_kernel(
    place_ref, early_ref, early_far_ref, late_ref, late_far_ref, rhs_ref, root_ref, idx_ref,
    placed_ref, out_ref, solved_ref, a_ref, c_ref, sem,
):
    here, core, sub, order = (place_ref[i] for i in range(4))
    s1, n = rhs_ref.shape
    q1 = s1 // ZL
    block = root_ref.shape[0]
    child_weights(here, core, (early_ref, early_far_ref), (late_ref, late_far_ref), a_ref, c_ref)
    rows = lax.broadcasted_iota(jnp.int32, (s1, n), 0)
    source = jnp.where(rows < order, rhs_ref[...], 0.0).astype(BF)
    for q in range(ZL):
        top = (q + 1) * q1
        part = dot(a_ref[q * q1 : top, :top], source[:top])
        part = jnp.where(rows[q * q1 : top] < order, part, 0.0)
        solved_ref[:, q * q1 : top] = part.T
    copy = pltpu.make_async_copy(solved_ref, out_ref, sem)
    copy.start()
    update = dot(solved_ref[...].astype(BF), c_ref[...], 1, 1).astype(BF)
    root = root_ref[...].T
    for b in range(placed_ref.shape[1] // block):
        part = dot(update, onehot(idx_ref, b * block, block))
        placed_ref[:, b * block : (b + 1) * block] = (
            jnp.where(sub == b, root, 0.0) - part
        ).astype(BF)
    copy.wait()


def root_kernel(
    place_ref, s_ref, early_ref, early_far_ref, late_ref, late_far_ref, out_ref, r_ref, f_ref
):
    here, core = place_ref[0], place_ref[1]
    s0 = s_ref.shape[1]
    q0 = s0 // ZL
    rc = early_ref.shape[1]

    def put(blocks_ref, steps, c):
        for j, step in enumerate(steps):
            y = lax.rem(here + (step + Y), Y)
            at = pl.multiple_of(y * (CORE * rc), CORE * rc) + c * rc
            r_ref[pl.ds(at, rc), :] = blocks_ref[j]

    by_core(core, (early_ref, early_far_ref), (late_ref, late_far_ref), put)
    left = 0
    spans = []
    for q in range(ZL):
        spans.append((left, left + s0 - q * q0))
        left = spans[-1][1]
    for q in range(ZL):
        term = dot(s_ref[:, q * q0 : (q + 1) * q0], r_ref[:, spans[q][0] : spans[q][1]])
        f_ref[:, q * q0 :] = term if q == 0 else f_ref[:, q * q0 :] + term
    f = f_ref[...].astype(BF)
    for q in range(ZL):
        part = dot(f[:, q * q0 :], r_ref[:, spans[q][0] : spans[q][1]], 1, 1).astype(BF)
        for i in range(out_ref.shape[0]):
            out_ref[i, :, q * q0 : (q + 1) * q0] = part


def backward_kernel(
    place_ref, x_ref, in_ref, early_ref, early_far_ref, late_ref, late_far_ref, idx_ref,
    out_ref, root_ref, solved_ref, a_ref, c_ref, sem,
):
    here, core, sub, order = (place_ref[i] for i in range(4))
    copy = pltpu.make_async_copy(in_ref, solved_ref, sem)
    copy.start()
    child_weights(here, core, (early_ref, early_far_ref), (late_ref, late_far_ref), a_ref, c_ref)
    n, s1 = solved_ref.shape
    q1 = s1 // ZL
    block = root_ref.shape[0]
    picked = None
    for b in range(x_ref.shape[1] // block):
        part = dot(x_ref[:, b * block : (b + 1) * block], onehot(idx_ref, b * block, block), 1, 1)
        picked = part if picked is None else picked + part
    pulled = dot(picked.astype(BF), c_ref[...])
    cols = lax.broadcasted_iota(jnp.int32, (n, s1), 1)
    copy.wait()
    residue = jnp.where(cols < order, solved_ref[...] - pulled, 0.0).astype(BF)
    rows = lax.broadcasted_iota(jnp.int32, (q1, n), 0)
    for q in range(ZL):
        part = dot(residue[:, q * q1 :], a_ref[q * q1 :, q * q1 : (q + 1) * q1])
        out_ref[q * q1 : (q + 1) * q1, :] = jnp.where(rows + q * q1 < order, part.T, 0.0)
    at = pl.multiple_of(sub * block, block)
    root_ref[...] = x_ref[:, pl.ds(at, block)].astype(F32).T


def pack_kernel(place_ref, r_ref, out_ref):
    block = r_ref.shape[4]
    left = 0
    for q in range(ZL):
        for x in range(q, X):
            for z in range(ZH):
                out_ref[:, left : left + block] = r_ref[x, z, q]
                left += block


def call(kernel, outs, args, scratch=(), flops=0, far=((), ())):
    moved = sum(a.size * a.dtype.itemsize for a in (*args, *outs))
    vmem = pl.BlockSpec(memory_space=pltpu.VMEM)
    hbm = pl.BlockSpec(memory_space=pltpu.HBM)
    return pl.pallas_call(
        kernel,
        out_shape=outs,
        in_specs=[pl.BlockSpec(memory_space=pltpu.SMEM)]
        + [hbm if i in far[0] else vmem for i in range(1, len(args))],
        out_specs=[hbm if i in far[1] else vmem for i in range(len(outs))],
        scratch_shapes=scratch,
        cost_estimate=pl.CostEstimate(flops=flops, transcendentals=0, bytes_accessed=moved),
        compiler_params=pltpu.CompilerParams(vmem_limit_bytes=20 << 20),
    )(*args)


def on_device(
    child_rhs, root_rhs, child_inverse, coupling_block, root_inverse, child_orders, coupling_rows
):
    n = child_rhs.shape[2]
    s1 = child_rhs.shape[1]
    q1 = s1 // ZL
    s0 = root_rhs.shape[0] * X * ZH
    q0 = s0 // ZL
    k = coupling_rows.shape[1]
    r1 = child_inverse.shape[1]
    block = root_rhs.shape[0]
    sub = lax.axis_index("x") * ZH + lax.axis_index("zh")
    place = jnp.stack([lax.axis_index("y"), lax.axis_index("core"), sub, child_orders[0]])
    idx = coupling_rows[0][:, None]
    shape = jax.ShapeDtypeStruct

    pair = jnp.concatenate([child_inverse[0], coupling_block[0]], axis=0)
    by_zl = gather_blocks(jnp.concatenate([pair, root_inverse.T], axis=1), "zl", ZL)
    own = jnp.concatenate(
        [by_zl[q, r1:, :s1] for q in range(ZL)]
        + [by_zl[q, :r1, : (q + 1) * q1] for q in reversed(range(ZL))],
        axis=1,
    )
    rt = after(by_zl[:, :, s1:], own)

    up = {1: lax.ppermute(own, "y", FORTH)}
    down = {1: lax.ppermute(own, "y", BACK)}
    rz = lax.ppermute(rt, "zh", SWAP)
    low = lax.axis_index("zh") == 0
    rt = jnp.stack([jnp.where(low, rt, rz), jnp.where(low, rz, rt)])
    up[2] = lax.ppermute(up[1], "y", FORTH)
    down[2] = lax.ppermute(down[1], "y", BACK)
    rt = gather_blocks(rt, "x", X)
    rwidth = block * ZH * sum(X - q for q in range(ZL))
    rt, = call(pack_kernel, [shape((rt.shape[3], rwidth), BF)], [place, rt])
    early = jnp.stack([own, up[1], down[1], up[2], down[2]])
    early_far = lax.ppermute(early, "core", SWAP)
    up[3] = lax.ppermute(up[2], "y", FORTH)
    down[3] = lax.ppermute(down[2], "y", BACK)
    up[4] = lax.ppermute(up[3], "y", FORTH)
    rt = after(rt, up[3], down[3])
    rup = {1: lax.ppermute(rt, "y", FORTH)}
    rdown = {1: lax.ppermute(rt, "y", BACK)}
    rup[2] = lax.ppermute(rup[1], "y", FORTH)
    rdown[2] = lax.ppermute(rdown[1], "y", BACK)
    last, ru, rd = lax.optimization_barrier((up[4], rup[1], rdown[1]))
    late = jnp.stack([up[3], down[3], last])
    late_far = lax.ppermute(late, "core", SWAP)

    weights = [early, early_far, late, late_far]
    scratch = [pltpu.VMEM((s1, s1), BF), pltpu.VMEM((k, s1), BF)]
    flops = 2 * n * (s1 * s1 + k * s1 + k * s0)
    placed, solved = call(
        forward_kernel,
        [shape((n, s0), BF), shape((n, s1), F32)],
        [place, *weights, child_rhs[0], root_rhs, idx],
        [pltpu.VMEM((n, s1), F32), *scratch, pltpu.SemaphoreType.DMA],
        flops,
        ((), (1,)),
    )
    rup[3] = lax.ppermute(after(rup[2], placed), "y", FORTH)
    rdown[3] = lax.ppermute(after(rdown[2], placed), "y", BACK)
    rearly = jnp.stack([rt, ru, rd, rup[2], rdown[2]])
    rearly_far = lax.ppermute(rearly, "core", SWAP)
    parts = lax.all_to_all(placed.reshape(X, n // X, s0), "x", 0, 0, tiled=True)
    part = jnp.sum(parts.astype(F32), axis=0)
    far = lax.ppermute(part.astype(BF), "zh", SWAP)
    rup[4] = lax.ppermute(rup[3], "y", FORTH)
    rlate = jnp.stack([rup[3], rdown[3], rup[4]])
    rlate_far = lax.ppermute(rlate, "core", SWAP)
    s_t = (part + far.astype(F32)).astype(BF)

    x_t, = call(
        root_kernel,
        [shape((X, n // X, s0), BF)],
        [place, s_t, rearly, rearly_far, rlate, rlate_far],
        [pltpu.VMEM((q0, rwidth), BF), pltpu.VMEM((n // X, s0), F32)],
        flops=4 * (n // X) * q0 * rwidth,
    )
    x_all = lax.all_to_all(x_t, "x", 0, 0, tiled=True).reshape(n, s0)

    child_out, root_out = call(
        backward_kernel,
        [shape((s1, n), F32), shape((block, n), F32)],
        [place, x_all, solved, *weights, idx],
        [pltpu.VMEM((n, s1), F32), *scratch, pltpu.SemaphoreType.DMA],
        flops,
        ((2,), ()),
    )
    return (child_out[None], root_out)


def solution(mesh):
    fine = Mesh(mesh.devices.reshape(ZL, Y, CORE, X, ZH), (*SRC, *SUB))
    return jax.shard_map(
        on_device,
        mesh=fine,
        in_specs=(
            P(SUB, None, SRC),
            P(SUB, SRC),
            P(SUB, SRC, None),
            P(SUB, SRC, None),
            P(SUB, SRC),
            P(SUB),
            P(SUB, None),
        ),
        out_specs=(P(SUB, None, SRC), P(SUB, SRC)),
        check_vma=False,
    )
```

```python
import jax
import jax.numpy as jnp
from jax import lax
from jax.experimental import pallas as pl
from jax.experimental.pallas import tpu as pltpu
from jax.sharding import Mesh, PartitionSpec as P

ZL, Y, CORE, X, ZH = 4, 8, 2, 4, 2
SRC = ("zl", "y", "core")
SUB = ("x", "zh")
BF = jnp.bfloat16
F32 = jnp.float32
FORTH = [(i, (i + 1) % Y) for i in range(Y)]
BACK = [(i, (i - 1) % Y) for i in range(Y)]
SWAP = [(0, 1), (1, 0)]
EARLY, LATE = (0, -1, 1, -2, 2), (-3, 3, -4)


def gather_blocks(x, axis, length):
    return lax.all_to_all(jnp.broadcast_to(x[None], (length, *x.shape)), axis, 0, 0, tiled=True)


def after(x, *others):
    return lax.optimization_barrier((x, *others))[0]


def dot(a, b, ca=1, cb=0):
    return lax.dot_general(a, b, (((ca,), (cb,)), ((), ())), preferred_element_type=F32)


def onehot(idx_ref, at, width):
    k = idx_ref.shape[0]
    cols = lax.broadcasted_iota(jnp.int32, (k, width), 1) + at
    return jnp.where(idx_ref[...] == cols, 1.0, 0.0).astype(BF)


def by_core(core, early, late, put):
    for mine, other in ((0, 1), (1, 0)):

        @pl.when(core == mine)
        def _():
            for blocks, steps in ((early, EARLY), (late, LATE)):
                put(blocks[0], steps, mine)
                put(blocks[1], steps, other)


def child_weights(here, core, early, late, a_ref, c_ref):
    s1 = a_ref.shape[0]
    r1 = early[0].shape[1]
    q1 = s1 // ZL

    def put(blocks_ref, steps, c):
        for j, step in enumerate(steps):
            y = lax.rem(here + (step + Y), Y)
            at = pl.multiple_of(y * (CORE * r1), CORE * r1) + c * r1
            for q in range(ZL):
                c_ref[pl.ds(q * q1 + at, r1), :] = blocks_ref[j, :, q * s1 : (q + 1) * s1]
            left = ZL * s1
            for q in reversed(range(ZL)):
                width = (q + 1) * q1
                a_ref[pl.ds(q * q1 + at, r1), :width] = blocks_ref[j, :, left : left + width]
                left += width

    by_core(core, early, late, put)


def forward_kernel(
    place_ref, early_ref, early_far_ref, late_ref, late_far_ref, rhs_ref, root_ref, idx_ref,
    placed_ref, out_ref, solved_ref, a_ref, c_ref, sem,
):
    here, core, sub, order = (place_ref[i] for i in range(4))
    s1, n = rhs_ref.shape
    q1 = s1 // ZL
    block = root_ref.shape[0]
    child_weights(here, core, (early_ref, early_far_ref), (late_ref, late_far_ref), a_ref, c_ref)
    rows = lax.broadcasted_iota(jnp.int32, (s1, n), 0)
    source = jnp.where(rows < order, rhs_ref[...], 0.0).astype(BF)
    for q in range(ZL):
        top = (q + 1) * q1
        part = dot(a_ref[q * q1 : top, :top], source[:top])
        part = jnp.where(rows[q * q1 : top] < order, part, 0.0)
        solved_ref[:, q * q1 : top] = part.T
    copy = pltpu.make_async_copy(solved_ref, out_ref, sem)
    copy.start()
    update = dot(solved_ref[...].astype(BF), c_ref[...], 1, 1).astype(BF)
    root = root_ref[...].T
    for b in range(placed_ref.shape[1] // block):
        part = dot(update, onehot(idx_ref, b * block, block))
        placed_ref[:, b * block : (b + 1) * block] = (
            jnp.where(sub == b, root, 0.0) - part
        ).astype(BF)
    copy.wait()


def root_kernel(place_ref, s_ref, mine_ref, other_ref, out_ref, r_ref, f_ref):
    core = place_ref[1]
    q0 = s_ref.shape[1] // ZL
    rc = mine_ref.shape[1]
    step = f_ref.shape[1] // ZL

    def put(blocks_ref, c):
        for y in range(Y):
            r_ref[(y * CORE + c) * rc : (y * CORE + c + 1) * rc, :] = blocks_ref[y]

    for mine in range(CORE):

        @pl.when(core == mine)
        def _():
            put(mine_ref, mine)
            put(other_ref, 1 - mine)

    spans = []
    for q in range(ZL):
        left = spans[-1][1] if q else 0
        spans.append((left, left + (X - q) * step))
    for q in range(ZL):
        term = dot(s_ref[:, q * q0 : (q + 1) * q0], r_ref[:, spans[q][0] : spans[q][1]])
        f_ref[:, q * step :] = term if q == 0 else f_ref[:, q * step :] + term
    f = f_ref[...].astype(BF)
    for q in range(ZL):
        out_ref[:, q * q0 : (q + 1) * q0] = dot(
            f[:, q * step :], r_ref[:, spans[q][0] : spans[q][1]], 1, 1
        )


def backward_kernel(
    place_ref, x_ref, in_ref, early_ref, early_far_ref, late_ref, late_far_ref, idx_ref,
    out_ref, root_ref, solved_ref, a_ref, c_ref, sem,
):
    here, core, sub, order = (place_ref[i] for i in range(4))
    copy = pltpu.make_async_copy(in_ref, solved_ref, sem)
    copy.start()
    child_weights(here, core, (early_ref, early_far_ref), (late_ref, late_far_ref), a_ref, c_ref)
    n, s1 = solved_ref.shape
    q1 = s1 // ZL
    block = root_ref.shape[0]
    picked = None
    for b in range(x_ref.shape[1] // block):
        part = dot(x_ref[:, b * block : (b + 1) * block], onehot(idx_ref, b * block, block), 1, 1)
        picked = part if picked is None else picked + part
    pulled = dot(picked.astype(BF), c_ref[...])
    cols = lax.broadcasted_iota(jnp.int32, (n, s1), 1)
    copy.wait()
    residue = jnp.where(cols < order, solved_ref[...] - pulled, 0.0).astype(BF)
    rows = lax.broadcasted_iota(jnp.int32, (q1, n), 0)
    for q in range(ZL):
        part = dot(residue[:, q * q1 :], a_ref[q * q1 :, q * q1 : (q + 1) * q1])
        out_ref[q * q1 : (q + 1) * q1, :] = jnp.where(rows + q * q1 < order, part.T, 0.0)
    at = pl.multiple_of(sub * block, block)
    root_ref[...] = x_ref[:, pl.ds(at, block)].astype(F32).T


def pack_kernel(place_ref, r_ref, out_ref):
    block = r_ref.shape[3]
    left = 0
    for q in range(ZL):
        for x in range(q, X):
            out_ref[:, left : left + block] = r_ref[x, q]
            left += block


def call(kernel, outs, args, scratch=(), flops=0, far=((), ())):
    moved = sum(a.size * a.dtype.itemsize for a in (*args, *outs))
    vmem = pl.BlockSpec(memory_space=pltpu.VMEM)
    hbm = pl.BlockSpec(memory_space=pltpu.HBM)
    return pl.pallas_call(
        kernel,
        out_shape=outs,
        in_specs=[pl.BlockSpec(memory_space=pltpu.SMEM)]
        + [hbm if i in far[0] else vmem for i in range(1, len(args))],
        out_specs=[hbm if i in far[1] else vmem for i in range(len(outs))],
        scratch_shapes=scratch,
        cost_estimate=pl.CostEstimate(flops=flops, transcendentals=0, bytes_accessed=moved),
        compiler_params=pltpu.CompilerParams(vmem_limit_bytes=20 << 20),
    )(*args)


def on_device(
    child_rhs, root_rhs, child_inverse, coupling_block, root_inverse, child_orders, coupling_rows
):
    n = child_rhs.shape[2]
    s1 = child_rhs.shape[1]
    q1 = s1 // ZL
    s0 = root_rhs.shape[0] * X * ZH
    q0 = s0 // ZL
    k = coupling_rows.shape[1]
    r1 = child_inverse.shape[1]
    block = root_rhs.shape[0]
    sub = lax.axis_index("x") * ZH + lax.axis_index("zh")
    place = jnp.stack([lax.axis_index("y"), lax.axis_index("core"), sub, child_orders[0]])
    idx = coupling_rows[0][:, None]
    shape = jax.ShapeDtypeStruct

    pair = jnp.concatenate([child_inverse[0], coupling_block[0]], axis=0)
    by_zl = gather_blocks(jnp.concatenate([pair, root_inverse.T], axis=1), "zl", ZL)
    own = jnp.concatenate(
        [by_zl[q, r1:, :s1] for q in range(ZL)]
        + [by_zl[q, :r1, : (q + 1) * q1] for q in reversed(range(ZL))],
        axis=1,
    )
    rt = after(by_zl[:, :, s1:], own)

    up = {1: lax.ppermute(own, "y", FORTH)}
    down = {1: lax.ppermute(own, "y", BACK)}
    rt = gather_blocks(rt, "x", X)
    rwidth = block * sum(X - q for q in range(ZL))
    rt, = call(pack_kernel, [shape((rt.shape[2], rwidth), BF)], [place, rt])
    up[2] = lax.ppermute(up[1], "y", FORTH)
    down[2] = lax.ppermute(down[1], "y", BACK)
    early = jnp.stack([own, up[1], down[1], up[2], down[2]])
    early_far = lax.ppermute(early, "core", SWAP)
    up[3] = lax.ppermute(up[2], "y", FORTH)
    down[3] = lax.ppermute(down[2], "y", BACK)
    up[4] = lax.ppermute(up[3], "y", FORTH)
    late = jnp.stack([up[3], down[3], up[4]])
    late_far = lax.ppermute(late, "core", SWAP)
    rmine = gather_blocks(after(rt, up[3], down[3]), "y", Y)

    weights = [early, early_far, late, late_far]
    scratch = [pltpu.VMEM((s1, s1), BF), pltpu.VMEM((k, s1), BF)]
    flops = 2 * n * (s1 * s1 + k * s1 + k * s0)
    placed, solved = call(
        forward_kernel,
        [shape((n, s0), BF), shape((n, s1), F32)],
        [place, *weights, child_rhs[0], root_rhs, idx],
        [pltpu.VMEM((n, s1), F32), *scratch, pltpu.SemaphoreType.DMA],
        flops,
        ((), (1,)),
    )
    here = lax.axis_index("x")
    blocks = placed.reshape(X, n // X, s0)
    block_for = lambda i: lax.dynamic_index_in_dim(blocks, lax.rem(here + i, X), 0, False)
    parts = [
        lax.ppermute(block_for(i), "x", [(j, (j + i) % X) for j in range(X)]) for i in (1, 3, 2)
    ]
    part = sum((p.astype(F32) for p in parts), block_for(0).astype(F32))
    rmine = after(rmine, part)
    rother = lax.ppermute(rmine, "core", SWAP)
    s_t = (part + lax.ppermute(part.astype(BF), "zh", SWAP).astype(F32)).astype(BF)

    x_part, = call(
        root_kernel,
        [shape((n // X, s0), F32)],
        [place, s_t, rmine, rother],
        [pltpu.VMEM((q0, rwidth), BF), pltpu.VMEM((n // X, s0 // ZH), F32)],
        4 * (n // X) * q0 * rwidth,
    )
    x_t = x_part + lax.ppermute(x_part.astype(BF), "zh", SWAP).astype(F32)
    x_all = gather_blocks(x_t.astype(BF), "x", X).reshape(n, s0)

    child_out, root_out = call(
        backward_kernel,
        [shape((s1, n), F32), shape((block, n), F32)],
        [place, x_all, solved, *weights, idx],
        [pltpu.VMEM((n, s1), F32), *scratch, pltpu.SemaphoreType.DMA],
        flops,
        ((2,), ()),
    )
    return (child_out[None], root_out)


def solution(mesh):
    fine = Mesh(mesh.devices.reshape(ZL, Y, CORE, X, ZH), (*SRC, *SUB))
    return jax.shard_map(
        on_device,
        mesh=fine,
        in_specs=(
            P(SUB, None, SRC),
            P(SUB, SRC),
            P(SUB, SRC, None),
            P(SUB, SRC, None),
            P(SUB, SRC),
            P(SUB),
            P(SUB, None),
        ),
        out_specs=(P(SUB, None, SRC), P(SUB, SRC)),
        check_vma=False,
    )
```

```python
import jax
import jax.numpy as jnp
from jax import lax
from jax.experimental import pallas as pl
from jax.experimental.pallas import tpu as pltpu
from jax.sharding import Mesh, PartitionSpec as P

ZL, Y, CORE, X, ZH = 4, 8, 2, 4, 2
SRC = ("zl", "y", "core")
SUB = ("x", "zh")
BF = jnp.bfloat16
F32 = jnp.float32
FORTH = [(i, (i + 1) % Y) for i in range(Y)]
BACK = [(i, (i - 1) % Y) for i in range(Y)]
SWAP = [(0, 1), (1, 0)]
EARLY, LATE = (0, -1, 1, -2, 2), (-3, 3, -4)


def gather_blocks(x, axis, length):
    return lax.all_to_all(jnp.broadcast_to(x[None], (length, *x.shape)), axis, 0, 0, tiled=True)


def after(x, *others):
    return lax.optimization_barrier((x, *others))[0]


def dot(a, b, ca=1, cb=0):
    return lax.dot_general(a, b, (((ca,), (cb,)), ((), ())), preferred_element_type=F32)


LANES = 128
FACTS = 5


def window(place_ref, idx_ref, b, block):
    k = idx_ref.shape[0]
    wide = min(k, block + LANES)
    start = jnp.minimum(place_ref[FACTS + b] // LANES * LANES, k - wide)
    at = pl.ds(pl.multiple_of(start, LANES), wide)
    cols = lax.broadcasted_iota(jnp.int32, (wide, block), 1) + b * block
    return at, jnp.where(idx_ref[at, :] == cols, 1.0, 0.0).astype(BF)


def by_core(core, early, late, put):
    for mine, other in ((0, 1), (1, 0)):

        @pl.when(core == mine)
        def _():
            for blocks, steps in ((early, EARLY), (late, LATE)):
                put(blocks[0], steps, mine)
                put(blocks[1], steps, other)


def start(sem, *pairs):
    copies = [pltpu.make_async_copy(a, b, sem.at[i]) for i, (a, b) in enumerate(pairs)]
    for copy in copies:
        copy.start()
    return copies


def child_weights(here, core, early, late, a_ref, c_ref):
    s1 = a_ref.shape[0]
    r1 = early[0].shape[1]
    q1 = s1 // ZL

    def put(blocks_ref, steps, c):
        for j, step in enumerate(steps):
            y = lax.rem(here + (step + Y), Y)
            at = pl.multiple_of(y * (CORE * r1), CORE * r1) + c * r1
            for q in range(ZL):
                c_ref[pl.ds(q * q1 + at, r1), :] = blocks_ref[j, :, q * s1 : (q + 1) * s1]
            left = ZL * s1
            for q in reversed(range(ZL)):
                width = (q + 1) * q1
                a_ref[pl.ds(q * q1 + at, r1), :width] = blocks_ref[j, :, left : left + width]
                left += width

    by_core(core, early, late, put)


def forward_kernel(
    place_ref, early_in_ref, early_far_in_ref, late_in_ref, late_far_in_ref, rhs_in_ref,
    root_in_ref, idx_ref, *refs,
):
    outs, solved_out_ref = refs[:X], refs[X]
    (
        a_ref, c_ref, early_ref, early_far_ref, late_ref, late_far_ref, solved_ref, rhs_ref, root_ref,
        update_ref, placed_ref, sem,
    ) = refs[X + 1 :]
    here, core, sub, order, x = (place_ref[i] for i in range(FACTS))
    loads = start(
        sem, (early_in_ref, early_ref), (early_far_in_ref, early_far_ref), (late_in_ref, late_ref),
        (late_far_in_ref, late_far_ref), (rhs_in_ref, rhs_ref), (root_in_ref, root_ref),
    )
    for load in loads[:4]:
        load.wait()
    s1, n = rhs_ref.shape
    q1 = s1 // ZL
    block = root_ref.shape[0]
    child_weights(here, core, (early_ref, early_far_ref), (late_ref, late_far_ref), a_ref, c_ref)
    for load in loads[4:]:
        load.wait()
    rows = lax.broadcasted_iota(jnp.int32, (s1, n), 0)
    source = jnp.where(rows < order, rhs_ref[...], 0.0).astype(BF)
    for q in range(ZL):
        top = (q + 1) * q1
        part = dot(a_ref[q * q1 : top, :top], source[:top])
        part = jnp.where(rows[q * q1 : top] < order, part, 0.0)
        solved_ref[:, q * q1 : top] = part.T
    store = pltpu.make_async_copy(solved_ref, solved_out_ref, sem.at[6])
    store.start()
    update_ref[...] = dot(solved_ref[...].astype(BF), c_ref[...], 1, 1).astype(BF)
    root = root_ref[...].T
    for b in range(placed_ref.shape[1] // block):
        at, hot = window(place_ref, idx_ref, b, block)
        placed_ref[:, b * block : (b + 1) * block] = (
            jnp.where(sub == b, root, 0.0) - dot(update_ref[:, at], hot)
        ).astype(BF)
    group = n // X
    for i, out_ref in enumerate(outs):
        at = pl.multiple_of(lax.rem(x + i, X) * group, group)
        out_ref[...] = placed_ref[pl.ds(at, group), :]
    store.wait()


def stack_kernel(place_ref, *refs):
    *blocks, out_ref, sem = refs
    copies = [
        pltpu.make_async_copy(ref, out_ref.at[i], sem.at[i]) for i, ref in enumerate(blocks)
    ]
    for copy in copies:
        copy.start()
    for copy in copies:
        copy.wait()


def sum_kernel(place_ref, a_ref, b_ref, c_ref, d_ref, out_ref):
    total = a_ref[...].astype(F32) + b_ref[...].astype(F32)
    total += c_ref[...].astype(F32) + d_ref[...].astype(F32)
    out_ref[...] = total.astype(BF)


def root_kernel(
    place_ref, near_ref, far_ref, mine_ref, other_ref, out_ref, sent_ref, r_ref, f_ref
):
    core = place_ref[1]
    s = (near_ref[...].astype(F32) + far_ref[...].astype(F32)).astype(BF)
    q0 = s.shape[1] // ZL
    rc = mine_ref.shape[1]
    step = f_ref.shape[1] // ZL

    def put(blocks_ref, c):
        for y in range(Y):
            r_ref[(y * CORE + c) * rc : (y * CORE + c + 1) * rc, :] = blocks_ref[y]

    for mine in range(CORE):

        @pl.when(core == mine)
        def _():
            put(mine_ref, mine)
            put(other_ref, 1 - mine)

    spans = []
    for q in range(ZL):
        left = spans[-1][1] if q else 0
        spans.append((left, left + (X - q) * step))
    for q in range(ZL):
        term = dot(s[:, q * q0 : (q + 1) * q0], r_ref[:, spans[q][0] : spans[q][1]])
        f_ref[:, q * step :] = term if q == 0 else f_ref[:, q * step :] + term
    f = f_ref[...].astype(BF)
    for q in range(ZL):
        part = dot(f[:, q * step :], r_ref[:, spans[q][0] : spans[q][1]], 1, 1)
        out_ref[:, q * q0 : (q + 1) * q0] = part
        sent_ref[:, q * q0 : (q + 1) * q0] = part.astype(BF)


def backward_kernel(
    place_ref, x_ref, in_ref, early_in_ref, early_far_in_ref, late_in_ref, late_far_in_ref, idx_ref,
    out_ref, root_ref, a_ref, c_ref, early_ref, early_far_ref, late_ref, late_far_ref, solved_ref,
    picked_ref, sem,
):
    here, core, sub, order = (place_ref[i] for i in range(4))
    *loads, copy = start(
        sem, (early_in_ref, early_ref), (early_far_in_ref, early_far_ref), (late_in_ref, late_ref),
        (late_far_in_ref, late_far_ref), (in_ref, solved_ref),
    )
    for load in loads:
        load.wait()
    child_weights(here, core, (early_ref, early_far_ref), (late_ref, late_far_ref), a_ref, c_ref)
    n, s1 = solved_ref.shape
    q1 = s1 // ZL
    block = root_ref.shape[0]
    picked_ref[...] = jnp.zeros_like(picked_ref)
    for b in range(x_ref.shape[1] // block):
        at, hot = window(place_ref, idx_ref, b, block)
        picked_ref[:, at] += dot(x_ref[:, b * block : (b + 1) * block], hot, 1, 1)
    pulled = dot(picked_ref[...].astype(BF), c_ref[...])
    cols = lax.broadcasted_iota(jnp.int32, (n, s1), 1)
    copy.wait()
    residue = jnp.where(cols < order, solved_ref[...] - pulled, 0.0).astype(BF)
    rows = lax.broadcasted_iota(jnp.int32, (q1, n), 0)
    for q in range(ZL):
        part = dot(residue[:, q * q1 :], a_ref[q * q1 :, q * q1 : (q + 1) * q1])
        out_ref[q * q1 : (q + 1) * q1, :] = jnp.where(rows + q * q1 < order, part.T, 0.0)
    at = pl.multiple_of(sub * block, block)
    root_ref[...] = x_ref[:, pl.ds(at, block)].astype(F32).T


def pack_kernel(place_ref, r_ref, out_ref):
    block = r_ref.shape[3]
    left = 0
    for q in range(ZL):
        for x in range(q, X):
            for y in range(Y):
                out_ref[y, :, left : left + block] = r_ref[x, q]
            left += block


def call(kernel, outs, args, scratch=(), flops=0, far=((), ())):
    moved = sum(a.size * a.dtype.itemsize for a in (*args, *outs))
    args = [
        pltpu.with_memory_space_constraint(a, pltpu.HBM) if i in far[0] else a
        for i, a in enumerate(args)
    ]
    outs = [pltpu.HBM(a.shape, a.dtype) if i in far[1] else a for i, a in enumerate(outs)]
    vmem = pl.BlockSpec(memory_space=pltpu.VMEM)
    hbm = pl.BlockSpec(memory_space=pltpu.HBM)
    return pl.pallas_call(
        kernel,
        out_shape=outs,
        in_specs=[pl.BlockSpec(memory_space=pltpu.SMEM)]
        + [hbm if i in far[0] else vmem for i in range(1, len(args))],
        out_specs=[hbm if i in far[1] else vmem for i in range(len(outs))],
        scratch_shapes=scratch,
        cost_estimate=pl.CostEstimate(flops=flops, transcendentals=0, bytes_accessed=moved),
        compiler_params=pltpu.CompilerParams(vmem_limit_bytes=20 << 20),
    )(*args)


def stack(place, *blocks):
    out = jax.ShapeDtypeStruct((len(blocks), *blocks[0].shape), blocks[0].dtype)
    sems = [pltpu.SemaphoreType.DMA((len(blocks),))]
    return call(stack_kernel, [out], [place, *blocks], sems, far=((), (0,)))[0]


def on_device(
    child_rhs, root_rhs, child_inverse, coupling_block, root_inverse, child_orders, coupling_rows
):
    n = child_rhs.shape[2]
    s1 = child_rhs.shape[1]
    q1 = s1 // ZL
    s0 = root_rhs.shape[0] * X * ZH
    q0 = s0 // ZL
    k = coupling_rows.shape[1]
    r1 = child_inverse.shape[1]
    block = root_rhs.shape[0]
    sub = lax.axis_index("x") * ZH + lax.axis_index("zh")
    idx = coupling_rows[0][:, None]
    edges = lax.iota(jnp.int32, s0 // block) * block
    below = jnp.sum((coupling_rows < edges[:, None]).astype(jnp.int32), axis=1)
    facts = [lax.axis_index("y"), lax.axis_index("core"), sub, child_orders[0], lax.axis_index("x")]
    place = jnp.concatenate([jnp.stack(facts), below])
    shape = jax.ShapeDtypeStruct

    pair = jnp.concatenate([child_inverse[0], coupling_block[0]], axis=0)
    by_zl = gather_blocks(jnp.concatenate([pair, root_inverse.T], axis=1), "zl", ZL)
    own = jnp.concatenate(
        [by_zl[q, r1:, :s1] for q in range(ZL)]
        + [by_zl[q, :r1, : (q + 1) * q1] for q in reversed(range(ZL))],
        axis=1,
    )
    rt = after(by_zl[:, :, s1:], own)

    up = {1: lax.ppermute(own, "y", FORTH)}
    down = {1: lax.ppermute(own, "y", BACK)}
    rt = gather_blocks(rt, "x", X)
    up[2] = lax.ppermute(up[1], "y", FORTH)
    down[2] = lax.ppermute(down[1], "y", BACK)
    rwidth = block * sum(X - q for q in range(ZL))
    rt = after(rt, up[2], down[2])
    rt, = call(pack_kernel, [shape((Y, rt.shape[2], rwidth), BF)], [place, rt])
    early = stack(place, own, up[1], down[1], up[2], down[2])
    early_far = lax.ppermute(early, "core", SWAP)
    up[3] = lax.ppermute(up[2], "y", FORTH)
    down[3] = lax.ppermute(down[2], "y", BACK)
    up[4] = lax.ppermute(up[3], "y", FORTH)
    late = stack(place, up[3], down[3], up[4])
    late_far = lax.ppermute(late, "core", SWAP)
    rmine = lax.all_to_all(after(rt, up[3], down[3]), "y", 0, 0, tiled=True)

    weights = [early, early_far, late, late_far]
    scratch = [pltpu.VMEM((s1, s1), BF), pltpu.VMEM((k, s1), BF)]
    scratch += [pltpu.VMEM(w.shape, BF) for w in weights] + [pltpu.VMEM((n, s1), F32)]
    flops = 2 * n * (s1 * s1 + k * s1 + k * s0)
    group = n // X
    *blocks, solved = call(
        forward_kernel,
        [shape((group, s0), BF)] * X + [shape((n, s1), F32)],
        [place, *weights, child_rhs[0], root_rhs, idx],
        [
            *scratch, pltpu.VMEM((s1, n), F32), pltpu.VMEM((block, n), F32),
            pltpu.VMEM((n, k), BF), pltpu.VMEM((n, s0), BF), pltpu.SemaphoreType.DMA((7,)),
        ],
        flops,
        ((1, 2, 3, 4, 5, 6), (X,)),
    )
    parts = [
        lax.ppermute(blocks[i], "x", [(j, (j + i) % X) for j in range(X)]) for i in (1, 3, 2)
    ]
    near, = call(sum_kernel, [shape((group, s0), BF)], [place, blocks[0], *parts])
    rmine = after(rmine, near)
    rother = lax.ppermute(rmine, "core", SWAP)
    far = lax.ppermute(near, "zh", SWAP)

    x_part, x_sent = call(
        root_kernel,
        [shape((group, s0), F32), shape((group, s0), BF)],
        [place, near, far, rmine, rother],
        [
            pltpu.VMEM((q0, rwidth), BF), pltpu.VMEM((group, s0 // ZH), F32),
        ],
        4 * group * q0 * rwidth,
    )
    x_t = x_part + lax.ppermute(x_sent, "zh", SWAP).astype(F32)
    x_all = gather_blocks(x_t.astype(BF), "x", X).reshape(n, s0)

    child_out, root_out = call(
        backward_kernel,
        [shape((s1, n), F32), shape((block, n), F32)],
        [place, x_all, solved, *weights, idx],
        [*scratch, pltpu.VMEM((n, k), F32), pltpu.SemaphoreType.DMA((5,))],
        flops,
        ((2, 3, 4, 5, 6), ()),
    )
    return (child_out[None], root_out)


def solution(mesh):
    fine = Mesh(mesh.devices.reshape(ZL, Y, CORE, X, ZH), (*SRC, *SUB))
    return jax.shard_map(
        on_device,
        mesh=fine,
        in_specs=(
            P(SUB, None, SRC),
            P(SUB, SRC),
            P(SUB, SRC, None),
            P(SUB, SRC, None),
            P(SUB, SRC),
            P(SUB),
            P(SUB, None),
        ),
        out_specs=(P(SUB, None, SRC), P(SUB, SRC)),
        check_vma=False,
    )
```

```python
import jax
import jax.numpy as jnp
from jax import lax
from jax.experimental import pallas as pl
from jax.experimental.pallas import tpu as pltpu
from jax.sharding import Mesh, PartitionSpec as P

ZL, Y, CORE, X, ZH = 4, 8, 2, 4, 2
SRC = ("zl", "y", "core")
SUB = ("x", "zh")
BF = jnp.bfloat16
F32 = jnp.float32
FORTH = [(i, (i + 1) % Y) for i in range(Y)]
BACK = [(i, (i - 1) % Y) for i in range(Y)]
SWAP = [(0, 1), (1, 0)]
EARLY, LATE = (0, -1, 1, -2, 2), (-3, 3, -4)


def gather_blocks(x, axis, length):
    return lax.all_to_all(jnp.broadcast_to(x[None], (length, *x.shape)), axis, 0, 0, tiled=True)


def after(x, *others):
    return lax.optimization_barrier((x, *others))[0]


def dot(a, b, ca=1, cb=0):
    return lax.dot_general(a, b, (((ca,), (cb,)), ((), ())), preferred_element_type=F32)


LANES = 128
FACTS = 5


def window(place_ref, idx_ref, b, block):
    k = idx_ref.shape[0]
    wide = min(k, block + LANES)
    start = jnp.minimum(place_ref[FACTS + b] // LANES * LANES, k - wide)
    at = pl.ds(pl.multiple_of(start, LANES), wide)
    cols = lax.broadcasted_iota(jnp.int32, (wide, block), 1) + b * block
    return at, jnp.where(idx_ref[at, :] == cols, 1.0, 0.0).astype(BF)


def by_core(core, early, late, put):
    for mine, other in ((0, 1), (1, 0)):

        @pl.when(core == mine)
        def _():
            for blocks, steps in ((early, EARLY), (late, LATE)):
                put(blocks[0], steps, mine)
                put(blocks[1], steps, other)


def start(sem, *pairs):
    copies = [pltpu.make_async_copy(a, b, sem.at[i]) for i, (a, b) in enumerate(pairs)]
    for copy in copies:
        copy.start()
    return copies


def child_weights(here, core, early, late, a_ref, c_ref):
    s1 = a_ref.shape[0]
    r1 = early[0].shape[1]
    q1 = s1 // ZL

    def put(blocks_ref, steps, c):
        for j, step in enumerate(steps):
            y = lax.rem(here + (step + Y), Y)
            at = pl.multiple_of(y * (CORE * r1), CORE * r1) + c * r1
            for q in range(ZL):
                c_ref[pl.ds(q * q1 + at, r1), :] = blocks_ref[j, :, q * s1 : (q + 1) * s1]
            left = ZL * s1
            for q in reversed(range(ZL)):
                width = (q + 1) * q1
                a_ref[pl.ds(q * q1 + at, r1), :width] = blocks_ref[j, :, left : left + width]
                left += width

    by_core(core, early, late, put)


def forward_kernel(
    place_ref, early_in_ref, early_far_in_ref, late_in_ref, late_far_in_ref, rhs_in_ref,
    root_in_ref, idx_ref, *refs,
):
    outs, solved_out_ref = refs[:X], refs[X]
    (
        a_ref, c_ref, early_ref, early_far_ref, late_ref, late_far_ref, solved_ref, rhs_ref, root_ref,
        update_ref, placed_ref, sem,
    ) = refs[X + 1 :]
    here, core, sub, order, x = (place_ref[i] for i in range(FACTS))
    loads = start(
        sem, (early_in_ref, early_ref), (early_far_in_ref, early_far_ref), (late_in_ref, late_ref),
        (late_far_in_ref, late_far_ref), (rhs_in_ref, rhs_ref), (root_in_ref, root_ref),
    )
    for load in loads[:4]:
        load.wait()
    s1, n = rhs_ref.shape
    q1 = s1 // ZL
    block = root_ref.shape[0]
    child_weights(here, core, (early_ref, early_far_ref), (late_ref, late_far_ref), a_ref, c_ref)
    for load in loads[4:]:
        load.wait()
    rows = lax.broadcasted_iota(jnp.int32, (s1, n), 0)
    source = jnp.where(rows < order, rhs_ref[...], 0.0).astype(BF)
    for q in range(ZL):
        top = (q + 1) * q1
        part = dot(a_ref[q * q1 : top, :top], source[:top])
        part = jnp.where(rows[q * q1 : top] < order, part, 0.0)
        solved_ref[:, q * q1 : top] = part.T
    store = pltpu.make_async_copy(solved_ref, solved_out_ref, sem.at[6])
    store.start()
    update_ref[...] = dot(solved_ref[...].astype(BF), c_ref[...], 1, 1).astype(BF)
    root = root_ref[...].T
    for b in range(placed_ref.shape[1] // block):
        at, hot = window(place_ref, idx_ref, b, block)
        placed_ref[:, b * block : (b + 1) * block] = (
            jnp.where(sub == b, root, 0.0) - dot(update_ref[:, at], hot)
        ).astype(BF)
    group = n // X
    for i, out_ref in enumerate(outs):
        at = pl.multiple_of(lax.rem(x + i, X) * group, group)
        out_ref[...] = placed_ref[pl.ds(at, group), :]
    store.wait()


def stack_kernel(place_ref, *refs):
    *blocks, out_ref, sem = refs
    copies = [
        pltpu.make_async_copy(ref, out_ref.at[i], sem.at[i]) for i, ref in enumerate(blocks)
    ]
    for copy in copies:
        copy.start()
    for copy in copies:
        copy.wait()


def sum_kernel(place_ref, a_ref, b_ref, c_ref, d_ref, out_ref):
    total = a_ref[...].astype(F32) + b_ref[...].astype(F32)
    total += c_ref[...].astype(F32) + d_ref[...].astype(F32)
    out_ref[...] = total.astype(BF)


def root_kernel(
    place_ref, near_ref, far_ref, mine_ref, other_ref, out_ref, sent_ref, r_ref, f_ref
):
    core = place_ref[1]
    s = (near_ref[...].astype(F32) + far_ref[...].astype(F32)).astype(BF)
    q0 = s.shape[1] // ZL
    rc = mine_ref.shape[1]
    step = f_ref.shape[1] // ZL

    def put(blocks_ref, c):
        for y in range(Y):
            r_ref[(y * CORE + c) * rc : (y * CORE + c + 1) * rc, :] = blocks_ref[y]

    for mine in range(CORE):

        @pl.when(core == mine)
        def _():
            put(mine_ref, mine)
            put(other_ref, 1 - mine)

    spans = []
    for q in range(ZL):
        left = spans[-1][1] if q else 0
        spans.append((left, left + (X - q) * step))
    for q in range(ZL):
        term = dot(s[:, q * q0 : (q + 1) * q0], r_ref[:, spans[q][0] : spans[q][1]])
        f_ref[:, q * step :] = term if q == 0 else f_ref[:, q * step :] + term
    f = f_ref[...].astype(BF)
    for q in range(ZL):
        part = dot(f[:, q * step :], r_ref[:, spans[q][0] : spans[q][1]], 1, 1)
        out_ref[:, q * q0 : (q + 1) * q0] = part
        sent_ref[:, q * q0 : (q + 1) * q0] = part.astype(BF)


def backward_kernel(
    place_ref, x_ref, in_ref, early_in_ref, early_far_in_ref, late_in_ref, late_far_in_ref, idx_ref,
    out_ref, root_ref, a_ref, c_ref, early_ref, early_far_ref, late_ref, late_far_ref, solved_ref,
    picked_ref, sem,
):
    here, core, sub, order = (place_ref[i] for i in range(4))
    *loads, copy = start(
        sem, (early_in_ref, early_ref), (early_far_in_ref, early_far_ref), (late_in_ref, late_ref),
        (late_far_in_ref, late_far_ref), (in_ref, solved_ref),
    )
    for load in loads:
        load.wait()
    child_weights(here, core, (early_ref, early_far_ref), (late_ref, late_far_ref), a_ref, c_ref)
    n, s1 = solved_ref.shape
    q1 = s1 // ZL
    block = root_ref.shape[0]
    picked_ref[...] = jnp.zeros_like(picked_ref)
    for b in range(x_ref.shape[1] // block):
        at, hot = window(place_ref, idx_ref, b, block)
        picked_ref[:, at] += dot(x_ref[:, b * block : (b + 1) * block], hot, 1, 1)
    pulled = dot(picked_ref[...].astype(BF), c_ref[...])
    cols = lax.broadcasted_iota(jnp.int32, (n, s1), 1)
    copy.wait()
    residue = jnp.where(cols < order, solved_ref[...] - pulled, 0.0).astype(BF)
    rows = lax.broadcasted_iota(jnp.int32, (q1, n), 0)
    for q in range(ZL):
        part = dot(residue[:, q * q1 :], a_ref[q * q1 :, q * q1 : (q + 1) * q1])
        out_ref[q * q1 : (q + 1) * q1, :] = jnp.where(rows + q * q1 < order, part.T, 0.0)
    at = pl.multiple_of(sub * block, block)
    root_ref[...] = x_ref[:, pl.ds(at, block)].astype(F32).T


def pack_kernel(place_ref, r_ref, out_ref):
    block = r_ref.shape[3]
    left = 0
    for q in range(ZL):
        for x in range(q, X):
            for y in range(Y):
                out_ref[y, :, left : left + block] = r_ref[x, q]
            left += block


def call(kernel, outs, args, scratch=(), flops=0, far=((), (), ())):
    moved = sum(a.size * a.dtype.itemsize for a in (*args, *outs))
    args = [
        pltpu.with_memory_space_constraint(a, pltpu.HBM) if i in far[0] and i not in far[2] else a
        for i, a in enumerate(args)
    ]
    outs = [pltpu.HBM(a.shape, a.dtype) if i in far[1] else a for i, a in enumerate(outs)]
    vmem = pl.BlockSpec(memory_space=pltpu.VMEM)
    hbm = pl.BlockSpec(memory_space=pltpu.HBM)
    return pl.pallas_call(
        kernel,
        out_shape=outs,
        in_specs=[pl.BlockSpec(memory_space=pltpu.SMEM)]
        + [hbm if i in far[0] else vmem for i in range(1, len(args))],
        out_specs=[hbm if i in far[1] else vmem for i in range(len(outs))],
        scratch_shapes=scratch,
        cost_estimate=pl.CostEstimate(flops=flops, transcendentals=0, bytes_accessed=moved),
        compiler_params=pltpu.CompilerParams(vmem_limit_bytes=20 << 20),
    )(*args)


def stack(place, *blocks):
    out = jax.ShapeDtypeStruct((len(blocks), *blocks[0].shape), blocks[0].dtype)
    sems = [pltpu.SemaphoreType.DMA((len(blocks),))]
    return call(stack_kernel, [out], [place, *blocks], sems, far=((), (0,), ()))[0]


def on_device(
    child_rhs, root_rhs, child_inverse, coupling_block, root_inverse, child_orders, coupling_rows
):
    n = child_rhs.shape[2]
    s1 = child_rhs.shape[1]
    q1 = s1 // ZL
    s0 = root_rhs.shape[0] * X * ZH
    q0 = s0 // ZL
    k = coupling_rows.shape[1]
    r1 = child_inverse.shape[1]
    block = root_rhs.shape[0]
    sub = lax.axis_index("x") * ZH + lax.axis_index("zh")
    idx = coupling_rows[0][:, None]
    edges = lax.iota(jnp.int32, s0 // block) * block
    below = jnp.sum((coupling_rows < edges[:, None]).astype(jnp.int32), axis=1)
    facts = [lax.axis_index("y"), lax.axis_index("core"), sub, child_orders[0], lax.axis_index("x")]
    place = jnp.concatenate([jnp.stack(facts), below])
    shape = jax.ShapeDtypeStruct

    pair = jnp.concatenate([child_inverse[0], coupling_block[0]], axis=0)
    by_zl = gather_blocks(jnp.concatenate([pair, root_inverse.T], axis=1), "zl", ZL)
    own = jnp.concatenate(
        [by_zl[q, r1:, :s1] for q in range(ZL)]
        + [by_zl[q, :r1, : (q + 1) * q1] for q in reversed(range(ZL))],
        axis=1,
    )
    rt = after(by_zl[:, :, s1:], own)

    both = lax.optimization_barrier
    up, down = both((lax.ppermute(own, "y", FORTH), lax.ppermute(own, "y", BACK)))
    first = (up, down)
    rt = gather_blocks(after(rt, up, down), "x", X)
    up, down = both((lax.ppermute(up, "y", FORTH), lax.ppermute(down, "y", BACK)))
    early = stack(place, own, *first, up, down)
    early_far = lax.ppermute(early, "core", SWAP)
    up, down = lax.ppermute(up, "y", FORTH), lax.ppermute(down, "y", BACK)
    up, down, rt, early_far = both((up, down, rt, early_far))
    last = lax.ppermute(up, "y", FORTH)
    rwidth = block * sum(X - q for q in range(ZL))
    rt, = call(pack_kernel, [shape((Y, rt.shape[2], rwidth), BF)], [place, rt])
    late = stack(place, up, down, last)
    late_far = lax.ppermute(late, "core", SWAP)
    rmine = lax.all_to_all(after(rt, late), "y", 0, 0, tiled=True)

    weights = [early, early_far, late, late_far]
    scratch = [pltpu.VMEM((s1, s1), BF), pltpu.VMEM((k, s1), BF)]
    scratch += [pltpu.VMEM(w.shape, BF) for w in weights] + [pltpu.VMEM((n, s1), F32)]
    flops = 2 * n * (s1 * s1 + k * s1 + k * s0)
    group = n // X
    *blocks, solved = call(
        forward_kernel,
        [shape((group, s0), BF)] * X + [shape((n, s1), F32)],
        [place, *weights, child_rhs[0], root_rhs, idx],
        [
            *scratch, pltpu.VMEM((s1, n), F32), pltpu.VMEM((block, n), F32),
            pltpu.VMEM((n, k), BF), pltpu.VMEM((n, s0), BF), pltpu.SemaphoreType.DMA((7,)),
        ],
        flops,
        ((1, 2, 3, 4, 5, 6), (X,), (4,)),
    )
    parts = [
        lax.ppermute(blocks[i], "x", [(j, (j + i) % X) for j in range(X)]) for i in (1, 3, 2)
    ]
    near, = call(sum_kernel, [shape((group, s0), BF)], [place, blocks[0], *parts])
    rmine = after(rmine, near)
    rother = lax.ppermute(rmine, "core", SWAP)
    far = lax.ppermute(near, "zh", SWAP)

    x_part, x_sent = call(
        root_kernel,
        [shape((group, s0), F32), shape((group, s0), BF)],
        [place, near, far, rmine, rother],
        [
            pltpu.VMEM((q0, rwidth), BF), pltpu.VMEM((group, s0 // ZH), F32),
        ],
        4 * group * q0 * rwidth,
    )
    x_t = x_part + lax.ppermute(x_sent, "zh", SWAP).astype(F32)
    x_all = gather_blocks(x_t.astype(BF), "x", X).reshape(n, s0)

    child_out, root_out = call(
        backward_kernel,
        [shape((s1, n), F32), shape((block, n), F32)],
        [place, x_all, solved, *weights, idx],
        [*scratch, pltpu.VMEM((n, k), F32), pltpu.SemaphoreType.DMA((5,))],
        flops,
        ((2, 3, 4, 5, 6), (), (6,)),
    )
    return (child_out[None], root_out)


def solution(mesh):
    fine = Mesh(mesh.devices.reshape(ZL, Y, CORE, X, ZH), (*SRC, *SUB))
    return jax.shard_map(
        on_device,
        mesh=fine,
        in_specs=(
            P(SUB, None, SRC),
            P(SUB, SRC),
            P(SUB, SRC, None),
            P(SUB, SRC, None),
            P(SUB, SRC),
            P(SUB),
            P(SUB, None),
        ),
        out_specs=(P(SUB, None, SRC), P(SUB, SRC)),
        check_vma=False,
    )
```

```python
import jax
import jax.numpy as jnp
from jax import lax
from jax.experimental import pallas as pl
from jax.experimental.pallas import tpu as pltpu
from jax.sharding import Mesh, PartitionSpec as P

ZL, Y, CORE, X, ZH = 4, 8, 2, 4, 2
SRC = ("zl", "y", "core")
SUB = ("x", "zh")
BF = jnp.bfloat16
F32 = jnp.float32
FORTH = [(i, (i + 1) % Y) for i in range(Y)]
BACK = [(i, (i - 1) % Y) for i in range(Y)]
SWAP = [(0, 1), (1, 0)]
EARLY, LATE = (0, -1, 1, -2, 2), (-3, 3, -4)


def gather_blocks(x, axis, length):
    return lax.all_to_all(jnp.broadcast_to(x[None], (length, *x.shape)), axis, 0, 0, tiled=True)


def after(x, *others):
    return lax.optimization_barrier((x, *others))[0]


def dot(a, b, ca=1, cb=0):
    return lax.dot_general(a, b, (((ca,), (cb,)), ((), ())), preferred_element_type=F32)


LANES = 128
FACTS = 5


def window(place_ref, idx_ref, b, block):
    k = idx_ref.shape[0]
    wide = min(k, block + LANES)
    start = jnp.minimum(place_ref[FACTS + b] // LANES * LANES, k - wide)
    at = pl.ds(pl.multiple_of(start, LANES), wide)
    cols = lax.broadcasted_iota(jnp.int32, (wide, block), 1) + b * block
    return at, jnp.where(idx_ref[at, :] == cols, 1.0, 0.0).astype(BF)


def by_core(core, early, late, put):
    for mine, other in ((0, 1), (1, 0)):

        @pl.when(core == mine)
        def _():
            for blocks, steps in ((early, EARLY), (late, LATE)):
                put(blocks[0], steps, mine)
                put(blocks[1], steps, other)


def start(sem, *pairs):
    copies = [pltpu.make_async_copy(a, b, sem.at[i]) for i, (a, b) in enumerate(pairs)]
    for copy in copies:
        copy.start()
    return copies


def child_weights(here, core, early, late, a_ref, c_ref):
    s1 = a_ref.shape[0]
    r1 = early[0].shape[1]
    q1 = s1 // ZL

    def put(blocks_ref, steps, c):
        for j, step in enumerate(steps):
            y = lax.rem(here + (step + Y), Y)
            at = pl.multiple_of(y * (CORE * r1), CORE * r1) + c * r1
            for q in range(ZL):
                c_ref[pl.ds(q * q1 + at, r1), :] = blocks_ref[j, :, q * s1 : (q + 1) * s1]
            left = ZL * s1
            for q in reversed(range(ZL)):
                width = (q + 1) * q1
                a_ref[pl.ds(q * q1 + at, r1), :width] = blocks_ref[j, :, left : left + width]
                left += width

    by_core(core, early, late, put)


def forward_kernel(
    place_ref, early_in_ref, early_far_in_ref, late_in_ref, late_far_in_ref, rhs_in_ref,
    root_in_ref, idx_ref, *refs,
):
    outs, solved_out_ref = refs[:X], refs[X]
    (
        a_ref, c_ref, early_ref, early_far_ref, late_ref, late_far_ref, solved_ref, rhs_ref, root_ref,
        update_ref, placed_ref, sem,
    ) = refs[X + 1 :]
    here, core, sub, order, x = (place_ref[i] for i in range(FACTS))
    loads = start(
        sem, (early_in_ref, early_ref), (early_far_in_ref, early_far_ref), (late_in_ref, late_ref),
        (late_far_in_ref, late_far_ref), (rhs_in_ref, rhs_ref), (root_in_ref, root_ref),
    )
    for load in loads[:4]:
        load.wait()
    s1, n = rhs_ref.shape
    q1 = s1 // ZL
    block = root_ref.shape[0]
    child_weights(here, core, (early_ref, early_far_ref), (late_ref, late_far_ref), a_ref, c_ref)
    for load in loads[4:]:
        load.wait()
    rows = lax.broadcasted_iota(jnp.int32, (s1, n), 0)
    source = jnp.where(rows < order, rhs_ref[...], 0.0).astype(BF)
    for q in range(ZL):
        top = (q + 1) * q1
        part = dot(a_ref[q * q1 : top, :top], source[:top])
        part = jnp.where(rows[q * q1 : top] < order, part, 0.0)
        solved_ref[:, q * q1 : top] = part.T
    store = pltpu.make_async_copy(solved_ref, solved_out_ref, sem.at[6])
    store.start()
    update_ref[...] = dot(solved_ref[...].astype(BF), c_ref[...], 1, 1).astype(BF)
    root = root_ref[...].T
    for b in range(placed_ref.shape[1] // block):
        at, hot = window(place_ref, idx_ref, b, block)
        placed_ref[:, b * block : (b + 1) * block] = (
            jnp.where(sub == b, root, 0.0) - dot(update_ref[:, at], hot)
        ).astype(BF)
    group = n // X
    for i, out_ref in enumerate(outs):
        at = pl.multiple_of(lax.rem(x + i, X) * group, group)
        out_ref[...] = placed_ref[pl.ds(at, group), :]
    store.wait()


def sum_kernel(place_ref, a_ref, b_ref, c_ref, d_ref, out_ref):
    total = a_ref[...].astype(F32) + b_ref[...].astype(F32)
    total += c_ref[...].astype(F32) + d_ref[...].astype(F32)
    out_ref[...] = total.astype(BF)


def root_kernel(
    place_ref, near_ref, far_ref, mine_ref, other_ref, out_ref, sent_ref, r_ref, f_ref
):
    core = place_ref[1]
    s = (near_ref[...].astype(F32) + far_ref[...].astype(F32)).astype(BF)
    q0 = s.shape[1] // ZL
    rc = mine_ref.shape[1]
    step = f_ref.shape[1] // ZL

    def put(blocks_ref, c):
        for y in range(Y):
            r_ref[(y * CORE + c) * rc : (y * CORE + c + 1) * rc, :] = blocks_ref[y]

    for mine in range(CORE):

        @pl.when(core == mine)
        def _():
            put(mine_ref, mine)
            put(other_ref, 1 - mine)

    spans = []
    for q in range(ZL):
        left = spans[-1][1] if q else 0
        spans.append((left, left + (X - q) * step))
    for q in range(ZL):
        term = dot(s[:, q * q0 : (q + 1) * q0], r_ref[:, spans[q][0] : spans[q][1]])
        f_ref[:, q * step :] = term if q == 0 else f_ref[:, q * step :] + term
    f = f_ref[...].astype(BF)
    for q in range(ZL):
        part = dot(f[:, q * step :], r_ref[:, spans[q][0] : spans[q][1]], 1, 1)
        out_ref[:, q * q0 : (q + 1) * q0] = part
        sent_ref[:, q * q0 : (q + 1) * q0] = part.astype(BF)


def backward_kernel(
    place_ref, x_ref, in_ref, early_in_ref, early_far_in_ref, late_in_ref, late_far_in_ref, idx_ref,
    out_ref, root_ref, a_ref, c_ref, early_ref, early_far_ref, late_ref, late_far_ref, solved_ref,
    picked_ref, sem,
):
    here, core, sub, order = (place_ref[i] for i in range(4))
    *loads, copy = start(
        sem, (early_in_ref, early_ref), (early_far_in_ref, early_far_ref), (late_in_ref, late_ref),
        (late_far_in_ref, late_far_ref), (in_ref, solved_ref),
    )
    for load in loads:
        load.wait()
    child_weights(here, core, (early_ref, early_far_ref), (late_ref, late_far_ref), a_ref, c_ref)
    n, s1 = solved_ref.shape
    q1 = s1 // ZL
    block = root_ref.shape[0]
    picked_ref[...] = jnp.zeros_like(picked_ref)
    for b in range(x_ref.shape[1] // block):
        at, hot = window(place_ref, idx_ref, b, block)
        picked_ref[:, at] += dot(x_ref[:, b * block : (b + 1) * block], hot, 1, 1)
    pulled = dot(picked_ref[...].astype(BF), c_ref[...])
    cols = lax.broadcasted_iota(jnp.int32, (n, s1), 1)
    copy.wait()
    residue = jnp.where(cols < order, solved_ref[...] - pulled, 0.0).astype(BF)
    rows = lax.broadcasted_iota(jnp.int32, (q1, n), 0)
    for q in range(ZL):
        part = dot(residue[:, q * q1 :], a_ref[q * q1 :, q * q1 : (q + 1) * q1])
        out_ref[q * q1 : (q + 1) * q1, :] = jnp.where(rows + q * q1 < order, part.T, 0.0)
    at = pl.multiple_of(sub * block, block)
    root_ref[...] = x_ref[:, pl.ds(at, block)].astype(F32).T


def pack_kernel(place_ref, r_ref, out_ref):
    block = r_ref.shape[3]
    left = 0
    for q in range(ZL):
        for x in range(q, X):
            out_ref[:, left : left + block] = r_ref[x, q]
            left += block


def call(kernel, outs, args, scratch=(), flops=0, far=((), (), ())):
    moved = sum(a.size * a.dtype.itemsize for a in (*args, *outs))
    args = [
        pltpu.with_memory_space_constraint(a, pltpu.HBM) if i in far[0] and i not in far[2] else a
        for i, a in enumerate(args)
    ]
    outs = [pltpu.HBM(a.shape, a.dtype) if i in far[1] else a for i, a in enumerate(outs)]
    vmem = pl.BlockSpec(memory_space=pltpu.VMEM)
    hbm = pl.BlockSpec(memory_space=pltpu.HBM)
    return pl.pallas_call(
        kernel,
        out_shape=outs,
        in_specs=[pl.BlockSpec(memory_space=pltpu.SMEM)]
        + [hbm if i in far[0] else vmem for i in range(1, len(args))],
        out_specs=[hbm if i in far[1] else vmem for i in range(len(outs))],
        scratch_shapes=scratch,
        cost_estimate=pl.CostEstimate(flops=flops, transcendentals=0, bytes_accessed=moved),
        compiler_params=pltpu.CompilerParams(vmem_limit_bytes=20 << 20),
    )(*args)


def on_device(
    child_rhs, root_rhs, child_inverse, coupling_block, root_inverse, child_orders, coupling_rows
):
    n = child_rhs.shape[2]
    s1 = child_rhs.shape[1]
    q1 = s1 // ZL
    s0 = root_rhs.shape[0] * X * ZH
    q0 = s0 // ZL
    k = coupling_rows.shape[1]
    r1 = child_inverse.shape[1]
    block = root_rhs.shape[0]
    sub = lax.axis_index("x") * ZH + lax.axis_index("zh")
    idx = coupling_rows[0][:, None]
    edges = lax.iota(jnp.int32, s0 // block) * block
    below = jnp.sum((coupling_rows < edges[:, None]).astype(jnp.int32), axis=1)
    facts = [lax.axis_index("y"), lax.axis_index("core"), sub, child_orders[0], lax.axis_index("x")]
    place = jnp.concatenate([jnp.stack(facts), below])
    shape = jax.ShapeDtypeStruct

    pair = jnp.concatenate([child_inverse[0], coupling_block[0]], axis=0)
    by_zl = gather_blocks(jnp.concatenate([pair, root_inverse.T], axis=1), "zl", ZL)
    own = jnp.concatenate(
        [by_zl[q, r1:, :s1] for q in range(ZL)]
        + [by_zl[q, :r1, : (q + 1) * q1] for q in reversed(range(ZL))],
        axis=1,
    )
    rt = after(by_zl[:, :, s1:], own)

    up = {1: lax.ppermute(own, "y", FORTH)}
    down = {1: lax.ppermute(own, "y", BACK)}
    rt = gather_blocks(rt, "x", X)
    rwidth = block * sum(X - q for q in range(ZL))
    rt, = call(pack_kernel, [shape((rt.shape[2], rwidth), BF)], [place, rt])
    up[2] = lax.ppermute(up[1], "y", FORTH)
    down[2] = lax.ppermute(down[1], "y", BACK)
    early = jnp.stack([own, up[1], down[1], up[2], down[2]])
    early_far = lax.ppermute(early, "core", SWAP)
    up[3] = lax.ppermute(up[2], "y", FORTH)
    down[3] = lax.ppermute(down[2], "y", BACK)
    up[4] = lax.ppermute(up[3], "y", FORTH)
    late = jnp.stack([up[3], down[3], up[4]])
    late_far = lax.ppermute(late, "core", SWAP)
    rmine = gather_blocks(after(rt, up[4]), "y", Y)

    weights = [early, early_far, late, late_far]
    scratch = [pltpu.VMEM((s1, s1), BF), pltpu.VMEM((k, s1), BF)]
    scratch += [pltpu.VMEM(w.shape, BF) for w in weights] + [pltpu.VMEM((n, s1), F32)]
    flops = 2 * n * (s1 * s1 + k * s1 + k * s0)
    group = n // X
    *blocks, solved = call(
        forward_kernel,
        [shape((group, s0), BF)] * X + [shape((n, s1), F32)],
        [place, *weights, child_rhs[0], root_rhs, idx],
        [
            *scratch, pltpu.VMEM((s1, n), F32), pltpu.VMEM((block, n), F32),
            pltpu.VMEM((n, k), BF), pltpu.VMEM((n, s0), BF), pltpu.SemaphoreType.DMA((7,)),
        ],
        flops,
        ((1, 2, 3, 4, 5, 6), (X,), (1, 2, 3, 4)),
    )
    parts = [
        lax.ppermute(blocks[i], "x", [(j, (j + i) % X) for j in range(X)]) for i in (1, 3, 2)
    ]
    near, = call(sum_kernel, [shape((group, s0), BF)], [place, blocks[0], *parts])
    rmine = after(rmine, near)
    rother = lax.ppermute(rmine, "core", SWAP)
    far = lax.ppermute(near, "zh", SWAP)

    x_part, x_sent = call(
        root_kernel,
        [shape((group, s0), F32), shape((group, s0), BF)],
        [place, near, far, rmine, rother],
        [
            pltpu.VMEM((q0, rwidth), BF), pltpu.VMEM((group, s0 // ZH), F32),
        ],
        4 * group * q0 * rwidth,
    )
    x_t = x_part + lax.ppermute(x_sent, "zh", SWAP).astype(F32)
    x_all = gather_blocks(x_t.astype(BF), "x", X).reshape(n, s0)

    child_out, root_out = call(
        backward_kernel,
        [shape((s1, n), F32), shape((block, n), F32)],
        [place, x_all, solved, *weights, idx],
        [*scratch, pltpu.VMEM((n, k), F32), pltpu.SemaphoreType.DMA((5,))],
        flops,
        ((2, 3, 4, 5, 6), (), (3, 4, 5, 6)),
    )
    return (child_out[None], root_out)


def solution(mesh):
    fine = Mesh(mesh.devices.reshape(ZL, Y, CORE, X, ZH), (*SRC, *SUB))
    return jax.shard_map(
        on_device,
        mesh=fine,
        in_specs=(
            P(SUB, None, SRC),
            P(SUB, SRC),
            P(SUB, SRC, None),
            P(SUB, SRC, None),
            P(SUB, SRC),
            P(SUB),
            P(SUB, None),
        ),
        out_specs=(P(SUB, None, SRC), P(SUB, SRC)),
        check_vma=False,
    )
```
